32 devices in a mesh: groups: 2 (over y), store: 16 (over z, x, core).
Axes of the slice: x: 2, y: 2, z: 4, core: 2. Of those that a mesh axis runs over, the one named last changes fastest.
Arguments:
- queries: bfloat16 [2, 32, 8192], P(None, ('groups', 'store')), parts along dimension 1, may hold values from -6 to 206
- new_keys: bfloat16 [2, 32, 1024], P(None, ('groups', 'store')), parts along dimension 1, may hold values from -6 to 12.5
- incoming_values: bfloat16 [2, 32, 1024], P(None, ('groups', 'store')), parts along dimension 1, may hold values from -6 to 6
- key_left: bfloat16 [32, 4096, 160], P(('groups', 'store')), parts along dimension 0, may hold values from -12 to 12
- right_key_factor: bfloat16 [32, 160, 1024], P(('groups', 'store')), parts along dimension 0, may hold values from -0.5 to 0.5
- value_tile_store: bfloat16 [131072, 1024], P(('groups', 'store')), parts along dimension 0, may hold values from -6 to 6
- slot_map: int32 [32, 8, 512], P(('groups', 'store')), parts along dimension 0, may hold values from 0 to 65535, as said below
- chosen: int32 [2, 32, 8, 64], P(None, ('groups', 'store')), parts along dimension 1, may hold values from 0 to 511, as said below
- lengths: int32 [32], P(('groups', 'store')), parts along dimension 0, may hold values from 1024 to 4096
Outputs:
- attended: bfloat16 [2, 32, 8192], P(None, ('groups', 'store')), parts along dimension 1
The draws below stay inside these ranges and needn't reach their ends.
There are 2 independent parts, one for each index of `groups`. The reference program is written for one: setup_inputs(seed, part) draws one part's arguments, and reference() takes and returns one part's arrays. A program takes and returns all parts, laid end to end along the dimension named above; each array names one. Nothing has to cross between parts.
Inputs may be any that keep to these rules, and one draw needn't show every extreme that they name: `slot_map`: the entries are distinct; pool rows r * 4096 to (r+1) * 4096 - 1 stand on index r of store. `chosen`: the 64 blocks of one step, request and key head are distinct; at most 8 of them have their slot_map row on one index of store, and in every step some index of store holds exactly 8 of them for every request and key head.
All inputs are finite; a program needn't handle non-finite values.
Results may differ from the reference program's by a relative error of at most 0.005.
The reference program's roundings to bfloat16 on the way count: a program that leaves them out, or rounds other values in their place, can miss the bound.
Values may be sent and summed in bfloat16 or wider, within the bound.
A program may use at most 64 MiB of HBM per device.

```python
import jax
import jax.numpy as jnp
from jax import lax

QUERY_HEADS = 64
KEY_VALUE_HEADS = 8
HEAD_SIZE = 128
FACTOR_RANK = 160
BLOCK_TOKENS = 8
SELECTED_BLOCKS = 64
DECODE_STEPS = 2
CTX = 4096
TOTAL_REQUESTS = 16
CACHE_BLOCKS = 512
PER_HOLDER = 8
DEVICE_TILES = 4096
POOL = 65536
N_STORE = 16


def layout(key):
    child_seed = jax.random.fold_in(key, 11)
    child_seeds = jax.random.split(child_seed, TOTAL_REQUESTS * KEY_VALUE_HEADS)
    tile_ordering = jax.vmap(lambda single: jax.random.permutation(single, CACHE_BLOCKS))(child_seeds)
    return tile_ordering.reshape(TOTAL_REQUESTS, KEY_VALUE_HEADS, CACHE_BLOCKS).astype(jnp.int32)


def draw_slot_map(key, part):
    tile_ordering = layout(key)
    device_share = CACHE_BLOCKS // N_STORE
    tile_keeper = tile_ordering // device_share
    inner_offset = tile_ordering % device_share
    row_ids = jnp.arange(TOTAL_REQUESTS, dtype=jnp.int32)[:, None, None]
    head_numbers = jnp.arange(KEY_VALUE_HEADS, dtype=jnp.int32)[None, :, None]
    canonical = (row_ids * KEY_VALUE_HEADS + head_numbers) * device_share + inner_offset
    holder_seeds = jax.random.split(jax.random.fold_in(key, 13), N_STORE)
    holder_orders = jax.vmap(lambda single: jax.random.permutation(single, DEVICE_TILES))(holder_seeds).astype(jnp.int32)
    placed = holder_orders[tile_keeper, canonical]
    return (tile_keeper * DEVICE_TILES + placed).astype(jnp.int32)


def draw_chosen(key, part):
    tile_ordering = layout(key)
    device_share = CACHE_BLOCKS // N_STORE
    tile_keeper = tile_ordering // device_share
    inner_offset = tile_ordering % device_share
    block_numbers = jnp.arange(CACHE_BLOCKS, dtype=jnp.int32)
    picks = []
    for step_index in range(DECODE_STEPS):
        step_key = jax.random.fold_in(key, 100 + step_index)
        heat_key, hot_key, noise_seed, window_key = jax.random.split(step_key, 4)
        window_start = jax.random.randint(window_key, (TOTAL_REQUESTS, KEY_VALUE_HEADS, N_STORE), 0, device_share).astype(jnp.int32)
        start_here = jnp.take_along_axis(window_start, tile_keeper, axis=2)
        eligible = (inner_offset - start_here + device_share) % device_share < PER_HOLDER
        heat_level = jax.random.randint(heat_key, (N_STORE,), 0, 4)
        hottest = jax.random.randint(hot_key, (), 0, N_STORE)
        heat_level = jnp.where(jnp.arange(N_STORE) == hottest, 16, heat_level)
        random_noise = jax.random.randint(noise_seed, (TOTAL_REQUESTS, KEY_VALUE_HEADS, CACHE_BLOCKS), 0, 4096)
        scores = jnp.where(eligible, (heat_level[tile_keeper] + 1) * (4096 * CACHE_BLOCKS) + random_noise * CACHE_BLOCKS + block_numbers, block_numbers)
        top_idx = lax.top_k(scores.astype(jnp.int32), SELECTED_BLOCKS)[1]
        picks.append(top_idx.astype(jnp.int32))
    return jnp.stack(picks)


def draw_queries(key, part):
    gaussian_seed = jax.random.fold_in(jax.random.fold_in(key, 21), 0)
    sampled_blocks = jnp.clip(jax.random.normal(gaussian_seed, (DECODE_STEPS, TOTAL_REQUESTS, QUERY_HEADS, HEAD_SIZE), jnp.float32), -6.0, 6.0)
    return sampled_blocks.reshape(DECODE_STEPS, TOTAL_REQUESTS, QUERY_HEADS * HEAD_SIZE).astype(jnp.bfloat16)


def draw_new_keys(key, part):
    gaussian_seed = jax.random.fold_in(jax.random.fold_in(key, 31), 0)
    sampled_blocks = jnp.clip(jax.random.normal(gaussian_seed, (DECODE_STEPS, TOTAL_REQUESTS, KEY_VALUE_HEADS, HEAD_SIZE), jnp.float32), -6.0, 6.0)
    sampled_blocks = jnp.clip(sampled_blocks, -6.0, 12.5)
    return sampled_blocks.reshape(DECODE_STEPS, TOTAL_REQUESTS, KEY_VALUE_HEADS * HEAD_SIZE).astype(jnp.bfloat16)


def touch_ends(entries, rng, low, largest):
    spot = [jax.random.randint(jax.random.fold_in(rng, axis), (), 0, length) for axis, length in enumerate(entries.shape)]
    longest = entries.shape.index(max(entries.shape))
    beside = spot[:longest] + [(spot[longest] + 1) % entries.shape[longest]] + spot[longest + 1:]
    return entries.at[tuple(spot)].set(low).at[tuple(beside)].set(largest)


def block_scale(key, dims, cuts, low, largest):
    def one(axis_at, shards_of):
        heights = jax.random.uniform(jax.random.fold_in(jax.random.fold_in(key, 6), axis_at), (shards_of,), jnp.float32, low / len(cuts), largest / len(cuts))
        return jnp.repeat(jnp.exp(heights), dims[axis_at] // shards_of).reshape((-1,) + (1,) * (len(dims) - axis_at - 1))

    factor_of = one(*cuts[0])
    for cut in cuts[1:]:
        factor_of = factor_of * one(*cut)
    return factor_of


def centred(stream_key, dims, deviation, bound, cuts=(), kind=jnp.bfloat16):
    result = jax.random.normal(stream_key, dims, jnp.float32) * deviation
    if len(cuts) > 0:
        result = block_scale(stream_key, dims, cuts, -0.22, 0.18) * result
    return jnp.clip(result, min=-bound, max=bound).astype(kind)


def setup_inputs(seed: int = 0, part: int = 0) -> dict:
    keys = jax.random.split(jax.random.key(seed), 10)
    own_keys = jax.random.split(jax.random.fold_in(keys[9], part), 10)
    queries = draw_queries(jax.random.fold_in(jax.random.fold_in(keys[9], part), 71), part)
    new_keys = draw_new_keys(jax.random.fold_in(jax.random.fold_in(keys[9], part), 71), part)
    incoming_values = centred(own_keys[2], (DECODE_STEPS, TOTAL_REQUESTS, KEY_VALUE_HEADS * HEAD_SIZE), 1.0, 6.0, ((1, 16),))
    key_left = centred(own_keys[3], (TOTAL_REQUESTS, CTX, FACTOR_RANK), 2.0, 12.0, ((0, 16),))
    right_key_factor = centred(own_keys[4], (TOTAL_REQUESTS, FACTOR_RANK, KEY_VALUE_HEADS * HEAD_SIZE), FACTOR_RANK ** -0.5, 0.5, ((0, 16),))
    value_tile_store = centred(own_keys[5], (POOL, BLOCK_TOKENS * HEAD_SIZE), 1.0, 6.0, ((0, 16),))
    slot_map = draw_slot_map(jax.random.fold_in(jax.random.fold_in(keys[9], part), 71), part)
    chosen = draw_chosen(jax.random.fold_in(jax.random.fold_in(keys[9], part), 71), part)
    lengths = touch_ends(jax.random.randint(own_keys[8], (TOTAL_REQUESTS,), CTX // 4, CTX + 1), jax.random.fold_in(own_keys[8], 1), CTX // 4, CTX).astype(jnp.int32)
    return {"queries": queries, "new_keys": new_keys, "incoming_values": incoming_values, "key_left": key_left, "right_key_factor": right_key_factor, "value_tile_store": value_tile_store, "slot_map": slot_map, "chosen": chosen, "lengths": lengths}


ROPE_BASE = 500000.0


def apply_rotary(tensor, token_positions):
    half_dim = tensor.shape[-1] // 2
    inverse = ROPE_BASE ** (-(jnp.arange(half_dim, dtype=jnp.float32) * 2.0 / tensor.shape[-1]))
    angles = jnp.asarray(token_positions).astype(jnp.float32)[..., None] * inverse
    cosine = jnp.cos(angles)
    sine_vals = jnp.sin(angles)
    first_half = tensor[..., :half_dim]
    second_half = tensor[..., half_dim:]
    return jnp.concatenate([first_half * cosine - second_half * sine_vals, second_half * cosine + first_half * sine_vals], -1)


def reference(queries, new_keys, incoming_values, key_left, right_key_factor, value_tile_store, slot_map, chosen, lengths):
    query_group_size = QUERY_HEADS // KEY_VALUE_HEADS
    score_scale = HEAD_SIZE ** -0.5

    def row_fn(per_row):
        query_full, incoming_keys_full, incoming_values_full, left_rows, right_factor_rows, slot_row, chosen_row, length = per_row
        right_factor_heads = right_factor_rows.reshape(FACTOR_RANK, KEY_VALUE_HEADS, HEAD_SIZE).astype(jnp.float32)
        results = []
        for step_index in range(DECODE_STEPS):
            block_numbers = chosen_row[step_index]
            token_positions = (block_numbers[:, :, None] * BLOCK_TOKENS + jnp.arange(BLOCK_TOKENS, dtype=jnp.int32)).reshape(KEY_VALUE_HEADS, SELECTED_BLOCKS * BLOCK_TOKENS)
            picked = left_rows[token_positions].astype(jnp.float32)
            raw_keys = jnp.einsum('htr,rhd->htd', picked, right_factor_heads)
            cache_keys = apply_rotary(raw_keys, token_positions).astype(jnp.bfloat16)
            rotated_query = apply_rotary(query_full[step_index].reshape(QUERY_HEADS, HEAD_SIZE).astype(jnp.float32), length + step_index).astype(jnp.bfloat16)
            current_position = (length + jnp.arange(step_index + 1, dtype=jnp.int32))[:, None]
            current_keys = apply_rotary(incoming_keys_full[:step_index + 1].reshape(step_index + 1, KEY_VALUE_HEADS, HEAD_SIZE).astype(jnp.float32), current_position).astype(jnp.bfloat16)
            current_keys = jnp.transpose(current_keys, (1, 0, 2))
            current_values = jnp.transpose(incoming_values_full[:step_index + 1].reshape(step_index + 1, KEY_VALUE_HEADS, HEAD_SIZE), (1, 0, 2))
            slot_numbers = jnp.take_along_axis(slot_row, block_numbers, axis=1)
            tile_row_index = value_tile_store[slot_numbers].reshape(KEY_VALUE_HEADS, SELECTED_BLOCKS * BLOCK_TOKENS, HEAD_SIZE)
            grouped_queries = rotated_query.reshape(KEY_VALUE_HEADS, query_group_size, HEAD_SIZE).astype(jnp.float32)
            cache_scores = jnp.einsum('hgd,htd->hgt', grouped_queries, cache_keys.astype(jnp.float32)) * score_scale
            inside_len = token_positions < length
            cache_scores = jnp.where(inside_len[:, None, :], cache_scores, -jnp.inf)
            fresh_scores = jnp.einsum('hgd,hnd->hgn', grouped_queries, current_keys.astype(jnp.float32)) * score_scale
            highest = jnp.maximum(jnp.max(cache_scores, -1, keepdims=True), jnp.max(fresh_scores, -1, keepdims=True))
            cache_exp = jnp.exp(cache_scores - highest)
            fresh_exp = jnp.exp(fresh_scores - highest)
            denominator = jnp.sum(cache_exp, -1, keepdims=True) + jnp.sum(fresh_exp, -1, keepdims=True)
            cache_weight = (cache_exp / denominator).astype(jnp.bfloat16)
            fresh_weight = (fresh_exp / denominator).astype(jnp.bfloat16)
            attended = jnp.einsum('hgt,htd->hgd', cache_weight.astype(jnp.float32), tile_row_index.astype(jnp.float32))
            attended = attended + jnp.einsum('hgn,hnd->hgd', fresh_weight.astype(jnp.float32), current_values.astype(jnp.float32))
            results.append(attended.reshape(QUERY_HEADS * HEAD_SIZE).astype(jnp.bfloat16))
        return jnp.stack(results)

    per_row = (jnp.transpose(queries, (1, 0, 2)), jnp.transpose(new_keys, (1, 0, 2)), jnp.transpose(incoming_values, (1, 0, 2)), key_left, right_key_factor, slot_map, jnp.transpose(chosen, (1, 0, 2, 3)), lengths)
    output = lax.map(row_fn, per_row)
    return jnp.transpose(output, (1, 0, 2))
```

```python
import functools

import jax
import jax.numpy as jnp
from jax import lax
from jax.experimental import pallas as pl
from jax.experimental.pallas import tpu as pltpu
from jax.sharding import PartitionSpec as P

KEY_VALUE_HEADS = 8
HEAD_SIZE = 128
BLOCK_TOKENS = 8


ROPE_BASE = 500000.0


def apply_rotary(tensor, token_positions):
    half_dim = tensor.shape[-1] // 2
    inverse = ROPE_BASE ** (-(jnp.arange(half_dim, dtype=jnp.float32) * 2.0 / tensor.shape[-1]))
    angles = jnp.asarray(token_positions).astype(jnp.float32)[..., None] * inverse
    cosine = jnp.cos(angles)
    sine_vals = jnp.sin(angles)
    first_half = tensor[..., :half_dim]
    second_half = tensor[..., half_dim:]
    return jnp.concatenate(
        [
            first_half * cosine - second_half * sine_vals,
            second_half * cosine + first_half * sine_vals,
        ],
        -1,
    )


def fetch_tiles(requests, value_tile_store):
    tile_row_index = jnp.take(
        value_tile_store,
        lax.all_to_all(requests, "store", split_axis=0, concat_axis=0, tiled=True),
        axis=0,
    )
    return lax.all_to_all(tile_row_index, "store", split_axis=0, concat_axis=0, tiled=True)


def build_requests(flat_idx, inside, total):
    buffer = jnp.zeros((total,), jnp.int32)
    return buffer.at[flat_idx.reshape(-1)].set(inside.reshape(-1))


def attend_row(
    query_full,
    incoming_keys_full,
    incoming_values_full,
    left_rows,
    right_factor_rows,
    block_numbers,
    tile_row_index,
    length,
    step_index,
):
    query_group_size = query_full.shape[-1] // HEAD_SIZE // KEY_VALUE_HEADS
    every_head = query_group_size * KEY_VALUE_HEADS
    selected_count = block_numbers.shape[1]
    score_scale = HEAD_SIZE ** (-0.5)
    right_factor_heads = right_factor_rows.reshape(
        right_factor_rows.shape[0], KEY_VALUE_HEADS, HEAD_SIZE
    )
    token_positions = (
        block_numbers[:, :, None] * BLOCK_TOKENS + jnp.arange(BLOCK_TOKENS, dtype=jnp.int32)
    ).reshape(KEY_VALUE_HEADS, selected_count * BLOCK_TOKENS)
    picked = left_rows[token_positions]
    raw_keys = jnp.einsum(
        "htr,rhd->htd", picked, right_factor_heads, preferred_element_type=jnp.float32
    )
    cache_keys = apply_rotary(raw_keys, token_positions).astype(jnp.bfloat16)
    rotated_query = apply_rotary(
        query_full[step_index].reshape(every_head, HEAD_SIZE).astype(jnp.float32),
        length + step_index,
    ).astype(jnp.bfloat16)
    current_position = (length + jnp.arange(step_index + 1, dtype=jnp.int32))[:, None]
    current_keys = apply_rotary(
        incoming_keys_full[: step_index + 1]
        .reshape(step_index + 1, KEY_VALUE_HEADS, HEAD_SIZE)
        .astype(jnp.float32),
        current_position,
    ).astype(jnp.bfloat16)
    current_keys = jnp.transpose(current_keys, (1, 0, 2))
    current_values = jnp.transpose(
        incoming_values_full[: step_index + 1].reshape(step_index + 1, KEY_VALUE_HEADS, HEAD_SIZE),
        (1, 0, 2),
    )
    local_values = tile_row_index.reshape(KEY_VALUE_HEADS, selected_count * BLOCK_TOKENS, HEAD_SIZE)
    grouped_queries = rotated_query.reshape(KEY_VALUE_HEADS, query_group_size, HEAD_SIZE)
    cache_scores = (
        jnp.einsum("hgd,htd->hgt", grouped_queries, cache_keys, preferred_element_type=jnp.float32)
        * score_scale
    )
    inside_len = token_positions < length
    cache_scores = jnp.where(inside_len[:, None, :], cache_scores, -jnp.inf)
    fresh_scores = (
        jnp.einsum(
            "hgd,hnd->hgn", grouped_queries, current_keys, preferred_element_type=jnp.float32
        )
        * score_scale
    )
    highest = jnp.maximum(
        jnp.max(cache_scores, -1, keepdims=True), jnp.max(fresh_scores, -1, keepdims=True)
    )
    cache_exp = jnp.exp(cache_scores - highest)
    fresh_exp = jnp.exp(fresh_scores - highest)
    denominator = jnp.sum(cache_exp, -1, keepdims=True) + jnp.sum(fresh_exp, -1, keepdims=True)
    cache_weight = (cache_exp / denominator).astype(jnp.bfloat16)
    fresh_weight = (fresh_exp / denominator).astype(jnp.bfloat16)
    attended = jnp.einsum(
        "hgt,htd->hgd", cache_weight, local_values, preferred_element_type=jnp.float32
    )
    attended = attended + jnp.einsum(
        "hgn,hnd->hgd", fresh_weight, current_values, preferred_element_type=jnp.float32
    )
    return attended.reshape(every_head * HEAD_SIZE).astype(jnp.bfloat16)


def per_device(
    queries,
    new_keys,
    incoming_values,
    key_left,
    right_key_factor,
    value_tile_store,
    slot_map,
    chosen,
    lengths,
):
    nstore = lax.axis_size("store")
    local_rows = key_left.shape[0]
    nchunk = slot_map.shape[2]
    step_count = chosen.shape[0]
    selected_count = chosen.shape[3]
    keeper_share = max(1, nchunk // nstore // 4)
    tile_limit = local_rows * KEY_VALUE_HEADS * keeper_share
    pool_here = value_tile_store.shape[0]
    slot_numbers = jnp.take_along_axis(
        jnp.broadcast_to(slot_map[None], (step_count,) + slot_map.shape), chosen, axis=3
    )
    tile_keeper = slot_numbers // pool_here
    inside = slot_numbers % pool_here
    matched = tile_keeper[..., :, None] == tile_keeper[..., None, :]
    earlier = jnp.arange(selected_count)[None, :] < jnp.arange(selected_count)[:, None]
    order_in = jnp.sum(jnp.logical_and(matched, earlier), -1)
    row_head = (
        jnp.arange(local_rows, dtype=jnp.int32)[:, None, None] * KEY_VALUE_HEADS
        + jnp.arange(KEY_VALUE_HEADS, dtype=jnp.int32)[None, :, None]
    )
    position = row_head * keeper_share + order_in
    tiles_all = []
    slot_span = step_count * tile_limit
    flat_idx = (
        tile_keeper * slot_span
        + jnp.arange(step_count, dtype=jnp.int32)[:, None, None, None] * tile_limit
        + position
    )
    requests = build_requests(flat_idx, inside, nstore * slot_span).reshape(nstore, slot_span)
    received = fetch_tiles(requests, value_tile_store).reshape(nstore * slot_span, -1)
    for step_index in range(step_count):
        tiles_all.append(received[flat_idx[step_index]])
    results = []
    for step_index in range(step_count):
        per_rows = [
            attend_row(
                queries[:, 0],
                new_keys[:, 0],
                incoming_values[:, 0],
                key_left[0],
                right_key_factor[0],
                chosen[step_index, 0],
                tiles_all[step_index][0],
                lengths[0],
                step_index,
            )
        ]
        results.append(jnp.stack(per_rows))
    return jnp.stack(results)


def plan_kernel(share, chosen_ref, keeper_ref, inside_ref, place_ref, request_ref):
    rows, picks = chosen_ref.shape
    heads, blocks = keeper_ref.shape
    total = request_ref.shape[1]
    holders = total // share
    block_at = lax.broadcasted_iota(jnp.int32, (rows, blocks), 1)
    chosen = chosen_ref[...]
    hit = jnp.zeros((rows, blocks), jnp.int32)
    for pick in range(picks):
        hit = jnp.where(chosen[:, pick : pick + 1] == block_at, 1, hit)
    keeper = jnp.concatenate([keeper_ref[...]] * (rows // heads), 0)
    kept = jnp.where(hit == 1, keeper, -1)
    before = (
        lax.broadcasted_iota(jnp.int32, (blocks, blocks), 0)
        < lax.broadcasted_iota(jnp.int32, (blocks, blocks), 1)
    ).astype(jnp.float32).astype(jnp.bfloat16)
    mine = [jnp.where(kept == holder, 1.0, 0.0) for holder in range(holders)]
    counts = jnp.dot(
        jnp.concatenate(mine, 0).astype(jnp.bfloat16), before, preferred_element_type=jnp.float32
    )
    order = jnp.zeros((rows, blocks), jnp.float32)
    for holder in range(holders):
        order = order + mine[holder] * counts[holder * rows : (holder + 1) * rows]
    place = jnp.where(hit == 1, keeper * share + order.astype(jnp.int32), -1)
    place_ref[...] = place
    inside = inside_ref[...]
    low = (inside & 255).astype(jnp.float32)
    middle = ((inside >> 8) & 255).astype(jnp.float32)
    high = (inside >> 16).astype(jnp.float32)
    slot_at = lax.broadcasted_iota(jnp.int32, (total, blocks), 0)
    for row in range(rows):
        head = row % heads
        digits = jnp.concatenate(
            [low[head : head + 1], middle[head : head + 1], high[head : head + 1],
             jnp.zeros((5, blocks), jnp.float32)], 0
        ).astype(jnp.bfloat16)
        table = jnp.where(place[row : row + 1] == slot_at, 1.0, 0.0).astype(jnp.bfloat16)
        found = lax.dot_general(
            digits, table, (((1,), (1,)), ((), ())), preferred_element_type=jnp.float32
        ).astype(jnp.int32)
        request_ref[row : row + 1, :] = found[0:1] + found[1:2] * 256 + found[2:3] * 65536


def weigh_kernel(
    share, length_ref, query_ref, fresh_key_ref, fresh_value_ref, left_ref, right_ref, place_ref,
    coarse_cos_ref, coarse_sin_ref, fine_cos_ref, fine_sin_ref,
    wire_ref, fresh_ref, cos_ref, sin_ref, sent_ref,
):
    head = pl.program_id(0)
    heads = pl.num_programs(0)
    in_block, blocks, _ = left_ref.shape
    steps = place_ref.shape[1]
    both = query_ref.shape[1]
    group = both // steps
    holders = wire_ref.shape[0]
    length = length_ref[0]

    @pl.when(head == 0)
    def _():
        coarse_cos = coarse_cos_ref[...][:, None, :]
        coarse_sin = coarse_sin_ref[...][:, None, :]
        sign = jnp.where(
            lax.broadcasted_iota(jnp.int32, (1, 1, HEAD_SIZE), 2) < HEAD_SIZE // 2, -1.0, 1.0
        )
        for j in range(in_block):
            fine_cos = fine_cos_ref[j][None]
            fine_sin = fine_sin_ref[j][None]
            cos_ref[j] = (coarse_cos * fine_cos - coarse_sin * fine_sin).reshape(blocks, HEAD_SIZE)
            sin_ref[j] = ((coarse_sin * fine_cos + coarse_cos * fine_sin) * sign).reshape(
                blocks, HEAD_SIZE
            )

    query = query_ref[0]
    place = place_ref[0]
    place_rows = jnp.concatenate(
        [jnp.broadcast_to(place[s : s + 1], (group, blocks)) for s in range(steps)], 0
    )
    block_at = lax.broadcasted_iota(jnp.int32, (both, blocks), 1)
    scale = HEAD_SIZE ** (-0.5)
    scores = []
    for j in range(in_block):
        raw = jnp.dot(left_ref[j], right_ref[...], preferred_element_type=jnp.float32)
        keys = (
            raw * cos_ref[j] + pltpu.roll(raw, HEAD_SIZE // 2, 1) * sin_ref[j]
        ).astype(jnp.bfloat16)
        score = lax.dot_general(
            query, keys, (((1,), (1,)), ((), ())), preferred_element_type=jnp.float32
        ) * scale
        keep = jnp.logical_and(place_rows >= 0, block_at * in_block + j < length)
        scores.append(jnp.where(keep, score, -jnp.inf))
    fresh = lax.dot_general(
        query, fresh_key_ref[0], (((1,), (1,)), ((), ())), preferred_element_type=jnp.float32
    ) * scale
    fresh_keep = (
        lax.broadcasted_iota(jnp.int32, fresh.shape, 1)
        <= lax.broadcasted_iota(jnp.int32, fresh.shape, 0) // group
    )
    fresh = jnp.where(fresh_keep, fresh, -jnp.inf)
    top = scores[0]
    for j in range(1, in_block):
        top = jnp.maximum(top, scores[j])
    highest = jnp.maximum(
        jnp.max(top, -1, keepdims=True), jnp.max(fresh, -1, keepdims=True)
    )
    powers = [jnp.exp(score - highest) for score in scores]
    fresh_power = jnp.exp(fresh - highest)
    total = powers[0]
    for j in range(1, in_block):
        total = total + powers[j]
    denominator = jnp.sum(total, -1, keepdims=True) + jnp.sum(fresh_power, -1, keepdims=True)
    weights = [power / denominator for power in powers]
    fresh_weight = (fresh_power / denominator).astype(jnp.bfloat16)
    fresh_ref[0] = jnp.dot(fresh_weight, fresh_value_ref[0], preferred_element_type=jnp.float32)
    slot_at = lax.broadcasted_iota(jnp.int32, (holders * share, blocks), 0)
    for s in range(steps):
        table = jnp.where(place[s : s + 1] == slot_at, 1.0, 0.0).astype(jnp.bfloat16)
        stacked = jnp.concatenate(
            [weight[s * group : (s + 1) * group] for weight in weights], 0
        ).astype(jnp.bfloat16)
        routed = lax.dot_general(
            table, stacked, (((1,), (1,)), ((), ())), preferred_element_type=jnp.float32
        )
        at = pl.multiple_of((s * heads + head) * share, share)
        sent_ref[:, pl.ds(at, share), :] = routed.reshape(holders, share, in_block * group)

    @pl.when(head == heads - 1)
    def _():
        for holder in range(holders):
            wire_ref[holder] = sent_ref[holder].T.astype(jnp.bfloat16)


def gather_kernel(share, weight_ref, tile_ref, part_ref):
    rows, lanes = part_ref.shape[1], weight_ref.shape[2]
    weight = weight_ref[0].astype(jnp.float32)
    in_block = tile_ref.shape[1] // HEAD_SIZE
    group = weight.shape[0] // in_block
    same = (
        lax.broadcasted_iota(jnp.int32, (rows, lanes), 0) // group
        == lax.broadcasted_iota(jnp.int32, (rows, lanes), 1) // share
    )
    total = jnp.zeros((rows, HEAD_SIZE), jnp.float32)
    for j in range(in_block):
        piece = weight[j * group : (j + 1) * group]
        spread = jnp.where(same, jnp.concatenate([piece] * (rows // group), 0), 0.0)
        total = total + jnp.dot(
            spread.astype(jnp.bfloat16),
            tile_ref[:, j * HEAD_SIZE : (j + 1) * HEAD_SIZE],
            preferred_element_type=jnp.float32,
        )
    part_ref[0] = total.astype(jnp.bfloat16)


def routed_device(
    queries, new_keys, incoming_values, key_left, right_key_factor, value_tile_store, slot_map,
    chosen, lengths,
):
    holders = lax.axis_size("store")
    steps, _, heads, picks = chosen.shape
    blocks = slot_map.shape[2]
    share = max(1, blocks // holders // 4)
    pool_here = value_tile_store.shape[0]
    group = queries.shape[2] // HEAD_SIZE // heads
    rank = key_left.shape[2]
    slots = steps * heads * share
    total = holders * share
    keeper = slot_map[0] // pool_here
    inside = slot_map[0] % pool_here
    place, request = pl.pallas_call(
        functools.partial(plan_kernel, share),
        out_shape=(
            jax.ShapeDtypeStruct((steps * heads, blocks), jnp.int32),
            jax.ShapeDtypeStruct((steps * heads, total), jnp.int32),
        ),
        name="plan",
    )(chosen[:, 0].reshape(steps * heads, picks), keeper, inside)
    request = request.reshape(steps * heads, holders, share).transpose(1, 0, 2)
    asked = lax.all_to_all(
        request.reshape(holders, slots), "store", split_axis=0, concat_axis=0, tiled=True
    )

    length = lengths[0]
    query = apply_rotary(
        queries[:, 0].reshape(steps, heads * group, HEAD_SIZE).astype(jnp.float32),
        (length + jnp.arange(steps, dtype=jnp.int32))[:, None],
    ).astype(jnp.bfloat16)
    query = query.reshape(steps, heads, group, HEAD_SIZE).transpose(1, 0, 2, 3)
    query = query.reshape(heads, steps * group, HEAD_SIZE)
    fresh_key = apply_rotary(
        new_keys[:, 0].reshape(steps, heads, HEAD_SIZE).astype(jnp.float32),
        (length + jnp.arange(steps, dtype=jnp.int32))[:, None],
    ).astype(jnp.bfloat16)
    extra = ((0, 0), (0, 8 - steps), (0, 0))
    fresh_key = jnp.pad(fresh_key.transpose(1, 0, 2), extra)
    fresh_value = jnp.pad(
        incoming_values[:, 0].reshape(steps, heads, HEAD_SIZE).transpose(1, 0, 2), extra
    )
    left = key_left[0].reshape(blocks, BLOCK_TOKENS, rank).transpose(1, 0, 2)

    half = HEAD_SIZE // 2
    inverse = ROPE_BASE ** (-(jnp.arange(half, dtype=jnp.float32) * 2.0 / HEAD_SIZE))
    inverse = jnp.concatenate([inverse, inverse])
    span = 8 * BLOCK_TOKENS
    coarse = (jnp.arange(blocks // 8, dtype=jnp.int32) * span).astype(jnp.float32)[:, None] * inverse
    fine = (
        jnp.arange(BLOCK_TOKENS, dtype=jnp.int32)[:, None]
        + jnp.arange(8, dtype=jnp.int32)[None, :] * BLOCK_TOKENS
    ).astype(jnp.float32)[..., None] * inverse
    whole = lambda *shape: pl.BlockSpec(shape, lambda h: (0,) * len(shape))
    per_head = lambda *shape: pl.BlockSpec((1,) + shape, lambda h: (h, 0, 0))
    wire, fresh = pl.pallas_call(
        functools.partial(weigh_kernel, share),
        grid=(heads,),
        in_specs=[
            pl.BlockSpec(memory_space=pltpu.SMEM),
            per_head(steps * group, HEAD_SIZE),
            per_head(8, HEAD_SIZE),
            per_head(8, HEAD_SIZE),
            whole(BLOCK_TOKENS, blocks, rank),
            pl.BlockSpec((rank, HEAD_SIZE), lambda h: (0, h)),
            per_head(steps, blocks),
            whole(blocks // 8, HEAD_SIZE),
            whole(blocks // 8, HEAD_SIZE),
            whole(BLOCK_TOKENS, 8, HEAD_SIZE),
            whole(BLOCK_TOKENS, 8, HEAD_SIZE),
        ],
        out_specs=(
            whole(holders, BLOCK_TOKENS * group, slots),
            per_head(steps * group, HEAD_SIZE),
        ),
        out_shape=(
            jax.ShapeDtypeStruct((holders, BLOCK_TOKENS * group, slots), jnp.bfloat16),
            jax.ShapeDtypeStruct((heads, steps * group, HEAD_SIZE), jnp.float32),
        ),
        scratch_shapes=[
            pltpu.VMEM((BLOCK_TOKENS, blocks, HEAD_SIZE), jnp.float32),
            pltpu.VMEM((BLOCK_TOKENS, blocks, HEAD_SIZE), jnp.float32),
            pltpu.VMEM((holders, slots, BLOCK_TOKENS * group), jnp.float32),
        ],
        cost_estimate=pl.CostEstimate(
            flops=4 * heads * blocks * BLOCK_TOKENS * rank * HEAD_SIZE,
            bytes_accessed=8 << 20,
            transcendentals=0,
        ),
        name="weigh",
    )(
        lengths, query, fresh_key, fresh_value, left, right_key_factor[0],
        place.reshape(steps, heads, blocks).transpose(1, 0, 2),
        jnp.cos(coarse), jnp.sin(coarse), jnp.cos(fine), jnp.sin(fine),
    )
    got = lax.all_to_all(wire, "store", split_axis=0, concat_axis=0, tiled=True)
    tiles = jnp.take(value_tile_store, asked.reshape(-1), axis=0)
    rows = steps * heads * group
    part = pl.pallas_call(
        functools.partial(gather_kernel, share),
        grid=(holders,),
        in_specs=[
            per_head(BLOCK_TOKENS * group, slots),
            pl.BlockSpec((slots, BLOCK_TOKENS * HEAD_SIZE), lambda h: (h, 0)),
        ],
        out_specs=per_head(rows, HEAD_SIZE),
        out_shape=jax.ShapeDtypeStruct((holders, rows, HEAD_SIZE), jnp.bfloat16),
        name="partial",
    )(got, tiles)
    back = lax.all_to_all(part, "store", split_axis=0, concat_axis=0, tiled=True)
    summed = jnp.sum(back.astype(jnp.float32), 0).reshape(steps, heads, group, HEAD_SIZE)
    fresh = fresh.reshape(heads, steps, group, HEAD_SIZE).transpose(1, 0, 2, 3)
    return (summed + fresh).astype(jnp.bfloat16).reshape(steps, 1, -1)


def solution(mesh):
    in_specs = (
        P(None, ("groups", "store"), None),
        P(None, ("groups", "store"), None),
        P(None, ("groups", "store"), None),
        P(("groups", "store"), None, None),
        P(("groups", "store"), None, None),
        P(("groups", "store"), None),
        P(("groups", "store"), None, None),
        P(None, ("groups", "store"), None, None),
        P(("groups", "store")),
    )
    out_specs = P(None, ("groups", "store"), None)
    def body(*args):
        share = max(1, args[6].shape[2] // mesh.shape["store"] // 4)
        return (routed_device if share == 8 else per_device)(*args)

    return jax.shard_map(
        body, mesh=mesh, in_specs=in_specs, out_specs=out_specs, check_vma=False
    )
```

```python
import functools

import jax
import jax.numpy as jnp
from jax import lax
from jax.experimental import pallas as pl
from jax.experimental.pallas import tpu as pltpu
from jax.sharding import PartitionSpec as P

KEY_VALUE_HEADS = 8
HEAD_SIZE = 128
BLOCK_TOKENS = 8


ROPE_BASE = 500000.0


def apply_rotary(tensor, token_positions):
    half_dim = tensor.shape[-1] // 2
    inverse = ROPE_BASE ** (-(jnp.arange(half_dim, dtype=jnp.float32) * 2.0 / tensor.shape[-1]))
    angles = jnp.asarray(token_positions).astype(jnp.float32)[..., None] * inverse
    cosine = jnp.cos(angles)
    sine_vals = jnp.sin(angles)
    first_half = tensor[..., :half_dim]
    second_half = tensor[..., half_dim:]
    return jnp.concatenate(
        [
            first_half * cosine - second_half * sine_vals,
            second_half * cosine + first_half * sine_vals,
        ],
        -1,
    )


def fetch_tiles(requests, value_tile_store):
    tile_row_index = jnp.take(
        value_tile_store,
        lax.all_to_all(requests, "store", split_axis=0, concat_axis=0, tiled=True),
        axis=0,
    )
    return lax.all_to_all(tile_row_index, "store", split_axis=0, concat_axis=0, tiled=True)


def build_requests(flat_idx, inside, total):
    buffer = jnp.zeros((total,), jnp.int32)
    return buffer.at[flat_idx.reshape(-1)].set(inside.reshape(-1))


def attend_row(
    query_full,
    incoming_keys_full,
    incoming_values_full,
    left_rows,
    right_factor_rows,
    block_numbers,
    tile_row_index,
    length,
    step_index,
):
    query_group_size = query_full.shape[-1] // HEAD_SIZE // KEY_VALUE_HEADS
    every_head = query_group_size * KEY_VALUE_HEADS
    selected_count = block_numbers.shape[1]
    score_scale = HEAD_SIZE ** (-0.5)
    right_factor_heads = right_factor_rows.reshape(
        right_factor_rows.shape[0], KEY_VALUE_HEADS, HEAD_SIZE
    )
    token_positions = (
        block_numbers[:, :, None] * BLOCK_TOKENS + jnp.arange(BLOCK_TOKENS, dtype=jnp.int32)
    ).reshape(KEY_VALUE_HEADS, selected_count * BLOCK_TOKENS)
    picked = left_rows[token_positions]
    raw_keys = jnp.einsum(
        "htr,rhd->htd", picked, right_factor_heads, preferred_element_type=jnp.float32
    )
    cache_keys = apply_rotary(raw_keys, token_positions).astype(jnp.bfloat16)
    rotated_query = apply_rotary(
        query_full[step_index].reshape(every_head, HEAD_SIZE).astype(jnp.float32),
        length + step_index,
    ).astype(jnp.bfloat16)
    current_position = (length + jnp.arange(step_index + 1, dtype=jnp.int32))[:, None]
    current_keys = apply_rotary(
        incoming_keys_full[: step_index + 1]
        .reshape(step_index + 1, KEY_VALUE_HEADS, HEAD_SIZE)
        .astype(jnp.float32),
        current_position,
    ).astype(jnp.bfloat16)
    current_keys = jnp.transpose(current_keys, (1, 0, 2))
    current_values = jnp.transpose(
        incoming_values_full[: step_index + 1].reshape(step_index + 1, KEY_VALUE_HEADS, HEAD_SIZE),
        (1, 0, 2),
    )
    local_values = tile_row_index.reshape(KEY_VALUE_HEADS, selected_count * BLOCK_TOKENS, HEAD_SIZE)
    grouped_queries = rotated_query.reshape(KEY_VALUE_HEADS, query_group_size, HEAD_SIZE)
    cache_scores = (
        jnp.einsum("hgd,htd->hgt", grouped_queries, cache_keys, preferred_element_type=jnp.float32)
        * score_scale
    )
    inside_len = token_positions < length
    cache_scores = jnp.where(inside_len[:, None, :], cache_scores, -jnp.inf)
    fresh_scores = (
        jnp.einsum(
            "hgd,hnd->hgn", grouped_queries, current_keys, preferred_element_type=jnp.float32
        )
        * score_scale
    )
    highest = jnp.maximum(
        jnp.max(cache_scores, -1, keepdims=True), jnp.max(fresh_scores, -1, keepdims=True)
    )
    cache_exp = jnp.exp(cache_scores - highest)
    fresh_exp = jnp.exp(fresh_scores - highest)
    denominator = jnp.sum(cache_exp, -1, keepdims=True) + jnp.sum(fresh_exp, -1, keepdims=True)
    cache_weight = (cache_exp / denominator).astype(jnp.bfloat16)
    fresh_weight = (fresh_exp / denominator).astype(jnp.bfloat16)
    attended = jnp.einsum(
        "hgt,htd->hgd", cache_weight, local_values, preferred_element_type=jnp.float32
    )
    attended = attended + jnp.einsum(
        "hgn,hnd->hgd", fresh_weight, current_values, preferred_element_type=jnp.float32
    )
    return attended.reshape(every_head * HEAD_SIZE).astype(jnp.bfloat16)


def per_device(
    queries,
    new_keys,
    incoming_values,
    key_left,
    right_key_factor,
    value_tile_store,
    slot_map,
    chosen,
    lengths,
):
    nstore = lax.axis_size("store")
    local_rows = key_left.shape[0]
    nchunk = slot_map.shape[2]
    step_count = chosen.shape[0]
    selected_count = chosen.shape[3]
    keeper_share = max(1, nchunk // nstore // 4)
    tile_limit = local_rows * KEY_VALUE_HEADS * keeper_share
    pool_here = value_tile_store.shape[0]
    slot_numbers = jnp.take_along_axis(
        jnp.broadcast_to(slot_map[None], (step_count,) + slot_map.shape), chosen, axis=3
    )
    tile_keeper = slot_numbers // pool_here
    inside = slot_numbers % pool_here
    matched = tile_keeper[..., :, None] == tile_keeper[..., None, :]
    earlier = jnp.arange(selected_count)[None, :] < jnp.arange(selected_count)[:, None]
    order_in = jnp.sum(jnp.logical_and(matched, earlier), -1)
    row_head = (
        jnp.arange(local_rows, dtype=jnp.int32)[:, None, None] * KEY_VALUE_HEADS
        + jnp.arange(KEY_VALUE_HEADS, dtype=jnp.int32)[None, :, None]
    )
    position = row_head * keeper_share + order_in
    tiles_all = []
    slot_span = step_count * tile_limit
    flat_idx = (
        tile_keeper * slot_span
        + jnp.arange(step_count, dtype=jnp.int32)[:, None, None, None] * tile_limit
        + position
    )
    requests = build_requests(flat_idx, inside, nstore * slot_span).reshape(nstore, slot_span)
    received = fetch_tiles(requests, value_tile_store).reshape(nstore * slot_span, -1)
    for step_index in range(step_count):
        tiles_all.append(received[flat_idx[step_index]])
    results = []
    for step_index in range(step_count):
        per_rows = [
            attend_row(
                queries[:, 0],
                new_keys[:, 0],
                incoming_values[:, 0],
                key_left[0],
                right_key_factor[0],
                chosen[step_index, 0],
                tiles_all[step_index][0],
                lengths[0],
                step_index,
            )
        ]
        results.append(jnp.stack(per_rows))
    return jnp.stack(results)


def plan_kernel(share, chosen_ref, keeper_ref, inside_ref, place_ref, request_ref):
    rows, picks = chosen_ref.shape
    heads, blocks = keeper_ref.shape
    total = request_ref.shape[1]
    holders = total // share
    block_at = lax.broadcasted_iota(jnp.int32, (rows, blocks), 1)
    chosen = chosen_ref[...]
    hit = jnp.zeros((rows, blocks), jnp.int32)
    for pick in range(picks):
        hit = jnp.where(chosen[:, pick : pick + 1] == block_at, 1, hit)
    keeper = jnp.concatenate([keeper_ref[...]] * (rows // heads), 0)
    kept = jnp.where(hit == 1, keeper, -1)
    before = (
        lax.broadcasted_iota(jnp.int32, (blocks, blocks), 0)
        < lax.broadcasted_iota(jnp.int32, (blocks, blocks), 1)
    ).astype(jnp.float32).astype(jnp.bfloat16)
    mine = [jnp.where(kept == holder, 1.0, 0.0) for holder in range(holders)]
    counts = jnp.dot(
        jnp.concatenate(mine, 0).astype(jnp.bfloat16), before, preferred_element_type=jnp.float32
    )
    order = jnp.zeros((rows, blocks), jnp.float32)
    for holder in range(holders):
        order = order + mine[holder] * counts[holder * rows : (holder + 1) * rows]
    place = jnp.where(hit == 1, keeper * share + order.astype(jnp.int32), -1)
    place_ref[...] = place
    inside = inside_ref[...]
    low = (inside & 255).astype(jnp.float32)
    middle = ((inside >> 8) & 255).astype(jnp.float32)
    high = (inside >> 16).astype(jnp.float32)
    slot_at = lax.broadcasted_iota(jnp.int32, (total, blocks), 0)
    for row in range(rows):
        head = row % heads
        digits = jnp.concatenate(
            [low[head : head + 1], middle[head : head + 1], high[head : head + 1],
             jnp.zeros((5, blocks), jnp.float32)], 0
        ).astype(jnp.bfloat16)
        table = jnp.where(place[row : row + 1] == slot_at, 1.0, 0.0).astype(jnp.bfloat16)
        found = lax.dot_general(
            digits, table, (((1,), (1,)), ((), ())), preferred_element_type=jnp.float32
        ).astype(jnp.int32)
        request_ref[row : row + 1, :] = found[0:1] + found[1:2] * 256 + found[2:3] * 65536


def weigh_kernel(
    share, length_ref, query_ref, fresh_key_ref, fresh_value_ref, left_ref, right_ref, place_ref,
    coarse_cos_ref, coarse_sin_ref, fine_cos_ref, fine_sin_ref,
    wire_ref, fresh_ref, cos_ref, sin_ref, sent_ref,
):
    head = pl.program_id(0)
    heads = pl.num_programs(0)
    in_block, blocks, _ = left_ref.shape
    steps = place_ref.shape[1]
    both = query_ref.shape[1]
    group = both // steps
    holders = wire_ref.shape[0]
    length = length_ref[0]

    @pl.when(head == 0)
    def _():
        coarse_cos = coarse_cos_ref[...][:, None, :]
        coarse_sin = coarse_sin_ref[...][:, None, :]
        sign = jnp.where(
            lax.broadcasted_iota(jnp.int32, (1, 1, HEAD_SIZE), 2) < HEAD_SIZE // 2, -1.0, 1.0
        )
        for j in range(in_block):
            fine_cos = fine_cos_ref[j][None]
            fine_sin = fine_sin_ref[j][None]
            cos_ref[j] = (coarse_cos * fine_cos - coarse_sin * fine_sin).reshape(blocks, HEAD_SIZE)
            sin_ref[j] = ((coarse_sin * fine_cos + coarse_cos * fine_sin) * sign).reshape(
                blocks, HEAD_SIZE
            )

    query = query_ref[0]
    place = place_ref[0]
    place_rows = jnp.concatenate(
        [jnp.broadcast_to(place[s : s + 1], (group, blocks)) for s in range(steps)], 0
    )
    block_at = lax.broadcasted_iota(jnp.int32, (both, blocks), 1)
    scale = HEAD_SIZE ** (-0.5)
    scores = []
    for j in range(in_block):
        raw = jnp.dot(left_ref[j], right_ref[...], preferred_element_type=jnp.float32)
        keys = (
            raw * cos_ref[j] + pltpu.roll(raw, HEAD_SIZE // 2, 1) * sin_ref[j]
        ).astype(jnp.bfloat16)
        score = lax.dot_general(
            query, keys, (((1,), (1,)), ((), ())), preferred_element_type=jnp.float32
        ) * scale
        keep = jnp.logical_and(place_rows >= 0, block_at * in_block + j < length)
        scores.append(jnp.where(keep, score, -jnp.inf))
    fresh = lax.dot_general(
        query, fresh_key_ref[0], (((1,), (1,)), ((), ())), preferred_element_type=jnp.float32
    ) * scale
    fresh_keep = (
        lax.broadcasted_iota(jnp.int32, fresh.shape, 1)
        <= lax.broadcasted_iota(jnp.int32, fresh.shape, 0) // group
    )
    fresh = jnp.where(fresh_keep, fresh, -jnp.inf)
    top = scores[0]
    for j in range(1, in_block):
        top = jnp.maximum(top, scores[j])
    highest = jnp.maximum(
        jnp.max(top, -1, keepdims=True), jnp.max(fresh, -1, keepdims=True)
    )
    powers = [jnp.exp(score - highest) for score in scores]
    fresh_power = jnp.exp(fresh - highest)
    total = powers[0]
    for j in range(1, in_block):
        total = total + powers[j]
    denominator = jnp.sum(total, -1, keepdims=True) + jnp.sum(fresh_power, -1, keepdims=True)
    weights = [power / denominator for power in powers]
    fresh_weight = (fresh_power / denominator).astype(jnp.bfloat16)
    fresh_ref[0] = jnp.dot(fresh_weight, fresh_value_ref[0], preferred_element_type=jnp.float32)
    slot_at = lax.broadcasted_iota(jnp.int32, (holders * share, blocks), 0)
    for s in range(steps):
        table = jnp.where(place[s : s + 1] == slot_at, 1.0, 0.0).astype(jnp.bfloat16)
        stacked = jnp.concatenate(
            [weight[s * group : (s + 1) * group] for weight in weights], 0
        ).astype(jnp.bfloat16)
        routed = lax.dot_general(
            table, stacked, (((1,), (1,)), ((), ())), preferred_element_type=jnp.float32
        )
        at = pl.multiple_of((s * heads + head) * share, share)
        sent_ref[:, pl.ds(at, share), :] = routed.reshape(holders, share, in_block * group)

    @pl.when(head == heads - 1)
    def _():
        for holder in range(holders):
            wire_ref[holder] = sent_ref[holder].T.astype(jnp.bfloat16)


def meet_kernel(
    share, wire_ref, fresh_ref, tiles_ref, out_ref,
    got_ref, part_ref, back_ref, block_ref,
    tile_sem, weight_send, weight_recv, part_send, part_recv,
):
    holders, lines, lanes = wire_ref.shape
    rows = out_ref.shape[0]
    in_block = block_ref.shape[2] // HEAD_SIZE
    group = lines // in_block
    me = lax.axis_index("store")

    def tile_copy(k):
        source = lax.rem(me - k + holders, holders)
        return pltpu.make_async_copy(
            tiles_ref.at[pl.ds(pl.multiple_of(source * lanes, lanes), lanes)],
            block_ref.at[k],
            tile_sem.at[k],
        )

    def weight_copy(k):
        peer = lax.rem(me + k, holders)
        return pltpu.make_async_remote_copy(
            src_ref=wire_ref.at[peer],
            dst_ref=got_ref.at[k],
            send_sem=weight_send.at[k],
            recv_sem=weight_recv.at[k],
            device_id={"store": peer},
            device_id_type=pl.DeviceIdType.MESH,
        )

    def part_copy(k):
        peer = lax.rem(me - k + holders, holders)
        return pltpu.make_async_remote_copy(
            src_ref=part_ref.at[k],
            dst_ref=back_ref.at[k],
            send_sem=part_send.at[k],
            recv_sem=part_recv.at[k],
            device_id={"store": peer},
            device_id_type=pl.DeviceIdType.MESH,
        )

    barrier = pltpu.get_barrier_semaphore()

    def greet(k, _):
        pl.semaphore_signal(
            barrier, inc=1, device_id={"store": lax.rem(me + k, holders)},
            device_id_type=pl.DeviceIdType.MESH,
        )
        return 0

    lax.fori_loop(1, holders, greet, 0)
    for k in range(holders):
        tile_copy(k).start()
    pl.semaphore_wait(barrier, holders - 1)
    for k in range(1, holders):
        weight_copy(k).start()

    same = (
        lax.broadcasted_iota(jnp.int32, (rows, lanes), 0) // group
        == lax.broadcasted_iota(jnp.int32, (rows, lanes), 1) // share
    )

    def partial(weight, k):
        total = jnp.zeros((rows, HEAD_SIZE), jnp.float32)
        weight = weight.astype(jnp.float32)
        for j in range(in_block):
            piece = weight[j * group : (j + 1) * group]
            spread = jnp.where(same, jnp.concatenate([piece] * (rows // group), 0), 0.0)
            total = total + jnp.dot(
                spread.astype(jnp.bfloat16),
                block_ref[k, :, j * HEAD_SIZE : (j + 1) * HEAD_SIZE],
                preferred_element_type=jnp.float32,
            )
        return total

    tile_copy(0).wait()
    own = partial(wire_ref[me], 0) + fresh_ref[...]

    def answer(k, _):
        tile_copy(k).wait()
        weight_copy(k).wait_recv()
        part_ref[k] = partial(got_ref[k], k).astype(jnp.bfloat16)
        part_copy(k).start()
        return 0

    lax.fori_loop(1, holders, answer, 0)

    def collect(k, total):
        part_copy(k).wait_recv()
        return total + back_ref[k].astype(jnp.float32)

    out_ref[...] = lax.fori_loop(1, holders, collect, own).astype(jnp.bfloat16)

    def finish(k, _):
        weight_copy(k).wait_send()
        part_copy(k).wait_send()
        return 0

    lax.fori_loop(1, holders, finish, 0)


def routed_device(
    queries, new_keys, incoming_values, key_left, right_key_factor, value_tile_store, slot_map,
    chosen, lengths,
):
    holders = lax.axis_size("store")
    steps, _, heads, picks = chosen.shape
    blocks = slot_map.shape[2]
    share = max(1, blocks // holders // 4)
    pool_here = value_tile_store.shape[0]
    group = queries.shape[2] // HEAD_SIZE // heads
    rank = key_left.shape[2]
    slots = steps * heads * share
    total = holders * share
    keeper = slot_map[0] // pool_here
    inside = slot_map[0] % pool_here
    place, request = pl.pallas_call(
        functools.partial(plan_kernel, share),
        out_shape=(
            jax.ShapeDtypeStruct((steps * heads, blocks), jnp.int32),
            jax.ShapeDtypeStruct((steps * heads, total), jnp.int32),
        ),
        name="plan",
    )(chosen[:, 0].reshape(steps * heads, picks), keeper, inside)
    request = request.reshape(steps * heads, holders, share).transpose(1, 0, 2)
    asked = lax.all_to_all(
        request.reshape(holders, slots), "store", split_axis=0, concat_axis=0, tiled=True
    )

    length = lengths[0]
    query = apply_rotary(
        queries[:, 0].reshape(steps, heads * group, HEAD_SIZE).astype(jnp.float32),
        (length + jnp.arange(steps, dtype=jnp.int32))[:, None],
    ).astype(jnp.bfloat16)
    query = query.reshape(steps, heads, group, HEAD_SIZE).transpose(1, 0, 2, 3)
    query = query.reshape(heads, steps * group, HEAD_SIZE)
    fresh_key = apply_rotary(
        new_keys[:, 0].reshape(steps, heads, HEAD_SIZE).astype(jnp.float32),
        (length + jnp.arange(steps, dtype=jnp.int32))[:, None],
    ).astype(jnp.bfloat16)
    extra = ((0, 0), (0, 8 - steps), (0, 0))
    fresh_key = jnp.pad(fresh_key.transpose(1, 0, 2), extra)
    fresh_value = jnp.pad(
        incoming_values[:, 0].reshape(steps, heads, HEAD_SIZE).transpose(1, 0, 2), extra
    )
    left = key_left[0].reshape(blocks, BLOCK_TOKENS, rank).transpose(1, 0, 2)

    half = HEAD_SIZE // 2
    inverse = ROPE_BASE ** (-(jnp.arange(half, dtype=jnp.float32) * 2.0 / HEAD_SIZE))
    inverse = jnp.concatenate([inverse, inverse])
    span = 8 * BLOCK_TOKENS
    coarse = (jnp.arange(blocks // 8, dtype=jnp.int32) * span).astype(jnp.float32)[:, None] * inverse
    fine = (
        jnp.arange(BLOCK_TOKENS, dtype=jnp.int32)[:, None]
        + jnp.arange(8, dtype=jnp.int32)[None, :] * BLOCK_TOKENS
    ).astype(jnp.float32)[..., None] * inverse
    whole = lambda *shape: pl.BlockSpec(shape, lambda h: (0,) * len(shape))
    per_head = lambda *shape: pl.BlockSpec((1,) + shape, lambda h: (h, 0, 0))
    wire, fresh = pl.pallas_call(
        functools.partial(weigh_kernel, share),
        grid=(heads,),
        in_specs=[
            pl.BlockSpec(memory_space=pltpu.SMEM),
            per_head(steps * group, HEAD_SIZE),
            per_head(8, HEAD_SIZE),
            per_head(8, HEAD_SIZE),
            whole(BLOCK_TOKENS, blocks, rank),
            pl.BlockSpec((rank, HEAD_SIZE), lambda h: (0, h)),
            per_head(steps, blocks),
            whole(blocks // 8, HEAD_SIZE),
            whole(blocks // 8, HEAD_SIZE),
            whole(BLOCK_TOKENS, 8, HEAD_SIZE),
            whole(BLOCK_TOKENS, 8, HEAD_SIZE),
        ],
        out_specs=(
            whole(holders, BLOCK_TOKENS * group, slots),
            per_head(steps * group, HEAD_SIZE),
        ),
        out_shape=(
            jax.ShapeDtypeStruct((holders, BLOCK_TOKENS * group, slots), jnp.bfloat16),
            jax.ShapeDtypeStruct((heads, steps * group, HEAD_SIZE), jnp.float32),
        ),
        scratch_shapes=[
            pltpu.VMEM((BLOCK_TOKENS, blocks, HEAD_SIZE), jnp.float32),
            pltpu.VMEM((BLOCK_TOKENS, blocks, HEAD_SIZE), jnp.float32),
            pltpu.VMEM((holders, slots, BLOCK_TOKENS * group), jnp.float32),
        ],
        cost_estimate=pl.CostEstimate(
            flops=4 * heads * blocks * BLOCK_TOKENS * rank * HEAD_SIZE,
            bytes_accessed=8 << 20,
            transcendentals=0,
        ),
        name="weigh",
    )(
        lengths, query, fresh_key, fresh_value, left, right_key_factor[0],
        place.reshape(steps, heads, blocks).transpose(1, 0, 2),
        jnp.cos(coarse), jnp.sin(coarse), jnp.cos(fine), jnp.sin(fine),
    )
    tiles = value_tile_store.at[asked.reshape(-1)].get(mode="promise_in_bounds")
    rows = steps * heads * group
    fresh = fresh.reshape(heads, steps, group, HEAD_SIZE).transpose(1, 0, 2, 3)
    lines = BLOCK_TOKENS * group
    in_vmem = pl.BlockSpec(memory_space=pltpu.VMEM)
    attended = pl.pallas_call(
        functools.partial(meet_kernel, share),
        in_specs=[in_vmem, in_vmem, pl.BlockSpec(memory_space=pl.ANY)],
        out_specs=in_vmem,
        out_shape=jax.ShapeDtypeStruct((rows, HEAD_SIZE), jnp.bfloat16),
        scratch_shapes=[
            pltpu.VMEM((holders, lines, slots), jnp.bfloat16),
            pltpu.VMEM((holders, rows, HEAD_SIZE), jnp.bfloat16),
            pltpu.VMEM((holders, rows, HEAD_SIZE), jnp.bfloat16),
            pltpu.VMEM((holders, slots, BLOCK_TOKENS * HEAD_SIZE), jnp.bfloat16),
        ]
        + [pltpu.SemaphoreType.DMA((holders,))] * 5,
        compiler_params=pltpu.CompilerParams(collective_id=0, has_side_effects=True),
        name="meet",
    )(wire, fresh.reshape(rows, HEAD_SIZE), tiles)
    return attended.reshape(steps, 1, -1)


def solution(mesh):
    in_specs = (
        P(None, ("groups", "store"), None),
        P(None, ("groups", "store"), None),
        P(None, ("groups", "store"), None),
        P(("groups", "store"), None, None),
        P(("groups", "store"), None, None),
        P(("groups", "store"), None),
        P(("groups", "store"), None, None),
        P(None, ("groups", "store"), None, None),
        P(("groups", "store")),
    )
    out_specs = P(None, ("groups", "store"), None)
    def body(*args):
        share = max(1, args[6].shape[2] // mesh.shape["store"] // 4)
        return (routed_device if share == 8 else per_device)(*args)

    return jax.shard_map(
        body, mesh=mesh, in_specs=in_specs, out_specs=out_specs, check_vma=False
    )
```

```python
import functools

import jax
import jax.numpy as jnp
import numpy as np
from jax import lax
from jax.experimental import pallas as pl
from jax.experimental.pallas import tpu as pltpu
from jax.sharding import PartitionSpec as P

KEY_VALUE_HEADS = 8
HEAD_SIZE = 128
BLOCK_TOKENS = 8


ROPE_BASE = 500000.0


def apply_rotary(tensor, token_positions):
    half_dim = tensor.shape[-1] // 2
    inverse = ROPE_BASE ** (-(jnp.arange(half_dim, dtype=jnp.float32) * 2.0 / tensor.shape[-1]))
    angles = jnp.asarray(token_positions).astype(jnp.float32)[..., None] * inverse
    cosine = jnp.cos(angles)
    sine_vals = jnp.sin(angles)
    first_half = tensor[..., :half_dim]
    second_half = tensor[..., half_dim:]
    return jnp.concatenate(
        [
            first_half * cosine - second_half * sine_vals,
            second_half * cosine + first_half * sine_vals,
        ],
        -1,
    )


def fetch_tiles(requests, value_tile_store):
    tile_row_index = jnp.take(
        value_tile_store,
        lax.all_to_all(requests, "store", split_axis=0, concat_axis=0, tiled=True),
        axis=0,
    )
    return lax.all_to_all(tile_row_index, "store", split_axis=0, concat_axis=0, tiled=True)


def build_requests(flat_idx, inside, total):
    buffer = jnp.zeros((total,), jnp.int32)
    return buffer.at[flat_idx.reshape(-1)].set(inside.reshape(-1))


def attend_row(
    query_full,
    incoming_keys_full,
    incoming_values_full,
    left_rows,
    right_factor_rows,
    block_numbers,
    tile_row_index,
    length,
    step_index,
):
    query_group_size = query_full.shape[-1] // HEAD_SIZE // KEY_VALUE_HEADS
    every_head = query_group_size * KEY_VALUE_HEADS
    selected_count = block_numbers.shape[1]
    score_scale = HEAD_SIZE ** (-0.5)
    right_factor_heads = right_factor_rows.reshape(
        right_factor_rows.shape[0], KEY_VALUE_HEADS, HEAD_SIZE
    )
    token_positions = (
        block_numbers[:, :, None] * BLOCK_TOKENS + jnp.arange(BLOCK_TOKENS, dtype=jnp.int32)
    ).reshape(KEY_VALUE_HEADS, selected_count * BLOCK_TOKENS)
    picked = left_rows[token_positions]
    raw_keys = jnp.einsum(
        "htr,rhd->htd", picked, right_factor_heads, preferred_element_type=jnp.float32
    )
    cache_keys = apply_rotary(raw_keys, token_positions).astype(jnp.bfloat16)
    rotated_query = apply_rotary(
        query_full[step_index].reshape(every_head, HEAD_SIZE).astype(jnp.float32),
        length + step_index,
    ).astype(jnp.bfloat16)
    current_position = (length + jnp.arange(step_index + 1, dtype=jnp.int32))[:, None]
    current_keys = apply_rotary(
        incoming_keys_full[: step_index + 1]
        .reshape(step_index + 1, KEY_VALUE_HEADS, HEAD_SIZE)
        .astype(jnp.float32),
        current_position,
    ).astype(jnp.bfloat16)
    current_keys = jnp.transpose(current_keys, (1, 0, 2))
    current_values = jnp.transpose(
        incoming_values_full[: step_index + 1].reshape(step_index + 1, KEY_VALUE_HEADS, HEAD_SIZE),
        (1, 0, 2),
    )
    local_values = tile_row_index.reshape(KEY_VALUE_HEADS, selected_count * BLOCK_TOKENS, HEAD_SIZE)
    grouped_queries = rotated_query.reshape(KEY_VALUE_HEADS, query_group_size, HEAD_SIZE)
    cache_scores = (
        jnp.einsum("hgd,htd->hgt", grouped_queries, cache_keys, preferred_element_type=jnp.float32)
        * score_scale
    )
    inside_len = token_positions < length
    cache_scores = jnp.where(inside_len[:, None, :], cache_scores, -jnp.inf)
    fresh_scores = (
        jnp.einsum(
            "hgd,hnd->hgn", grouped_queries, current_keys, preferred_element_type=jnp.float32
        )
        * score_scale
    )
    highest = jnp.maximum(
        jnp.max(cache_scores, -1, keepdims=True), jnp.max(fresh_scores, -1, keepdims=True)
    )
    cache_exp = jnp.exp(cache_scores - highest)
    fresh_exp = jnp.exp(fresh_scores - highest)
    denominator = jnp.sum(cache_exp, -1, keepdims=True) + jnp.sum(fresh_exp, -1, keepdims=True)
    cache_weight = (cache_exp / denominator).astype(jnp.bfloat16)
    fresh_weight = (fresh_exp / denominator).astype(jnp.bfloat16)
    attended = jnp.einsum(
        "hgt,htd->hgd", cache_weight, local_values, preferred_element_type=jnp.float32
    )
    attended = attended + jnp.einsum(
        "hgn,hnd->hgd", fresh_weight, current_values, preferred_element_type=jnp.float32
    )
    return attended.reshape(every_head * HEAD_SIZE).astype(jnp.bfloat16)


def per_device(
    queries,
    new_keys,
    incoming_values,
    key_left,
    right_key_factor,
    value_tile_store,
    slot_map,
    chosen,
    lengths,
):
    nstore = lax.axis_size("store")
    local_rows = key_left.shape[0]
    nchunk = slot_map.shape[2]
    step_count = chosen.shape[0]
    selected_count = chosen.shape[3]
    keeper_share = max(1, nchunk // nstore // 4)
    tile_limit = local_rows * KEY_VALUE_HEADS * keeper_share
    pool_here = value_tile_store.shape[0]
    slot_numbers = jnp.take_along_axis(
        jnp.broadcast_to(slot_map[None], (step_count,) + slot_map.shape), chosen, axis=3
    )
    tile_keeper = slot_numbers // pool_here
    inside = slot_numbers % pool_here
    matched = tile_keeper[..., :, None] == tile_keeper[..., None, :]
    earlier = jnp.arange(selected_count)[None, :] < jnp.arange(selected_count)[:, None]
    order_in = jnp.sum(jnp.logical_and(matched, earlier), -1)
    row_head = (
        jnp.arange(local_rows, dtype=jnp.int32)[:, None, None] * KEY_VALUE_HEADS
        + jnp.arange(KEY_VALUE_HEADS, dtype=jnp.int32)[None, :, None]
    )
    position = row_head * keeper_share + order_in
    tiles_all = []
    slot_span = step_count * tile_limit
    flat_idx = (
        tile_keeper * slot_span
        + jnp.arange(step_count, dtype=jnp.int32)[:, None, None, None] * tile_limit
        + position
    )
    requests = build_requests(flat_idx, inside, nstore * slot_span).reshape(nstore, slot_span)
    received = fetch_tiles(requests, value_tile_store).reshape(nstore * slot_span, -1)
    for step_index in range(step_count):
        tiles_all.append(received[flat_idx[step_index]])
    results = []
    for step_index in range(step_count):
        per_rows = [
            attend_row(
                queries[:, 0],
                new_keys[:, 0],
                incoming_values[:, 0],
                key_left[0],
                right_key_factor[0],
                chosen[step_index, 0],
                tiles_all[step_index][0],
                lengths[0],
                step_index,
            )
        ]
        results.append(jnp.stack(per_rows))
    return jnp.stack(results)


def plan_kernel(share, chosen_ref, keeper_ref, inside_ref, place_ref, request_ref):
    rows, picks = chosen_ref.shape
    heads, blocks = keeper_ref.shape
    total = request_ref.shape[1]
    holders = total // share
    block_at = lax.broadcasted_iota(jnp.int32, (rows, blocks), 1)
    chosen = chosen_ref[...]
    hit = jnp.zeros((rows, blocks), jnp.int32)
    for pick in range(picks):
        hit = jnp.where(chosen[:, pick : pick + 1] == block_at, 1, hit)
    keeper = jnp.concatenate([keeper_ref[...]] * (rows // heads), 0)
    kept = jnp.where(hit == 1, keeper, -1)
    before = (
        lax.broadcasted_iota(jnp.int32, (blocks, blocks), 0)
        < lax.broadcasted_iota(jnp.int32, (blocks, blocks), 1)
    ).astype(jnp.float32).astype(jnp.bfloat16)
    mine = [jnp.where(kept == holder, 1.0, 0.0) for holder in range(holders)]
    counts = jnp.dot(
        jnp.concatenate(mine, 0).astype(jnp.bfloat16), before, preferred_element_type=jnp.float32
    )
    order = jnp.zeros((rows, blocks), jnp.float32)
    for holder in range(holders):
        order = order + mine[holder] * counts[holder * rows : (holder + 1) * rows]
    place = jnp.where(hit == 1, keeper * share + order.astype(jnp.int32), -1)
    place_ref[...] = place
    inside = inside_ref[...]
    low = (inside & 255).astype(jnp.float32)
    middle = ((inside >> 8) & 255).astype(jnp.float32)
    high = (inside >> 16).astype(jnp.float32)
    slot_at = lax.broadcasted_iota(jnp.int32, (total, blocks), 0)
    for row in range(rows):
        head = row % heads
        digits = jnp.concatenate(
            [low[head : head + 1], middle[head : head + 1], high[head : head + 1],
             jnp.zeros((5, blocks), jnp.float32)], 0
        ).astype(jnp.bfloat16)
        table = jnp.where(place[row : row + 1] == slot_at, 1.0, 0.0).astype(jnp.bfloat16)
        found = lax.dot_general(
            digits, table, (((1,), (1,)), ((), ())), preferred_element_type=jnp.float32
        ).astype(jnp.int32)
        request_ref[row : row + 1, :] = found[0:1] + found[1:2] * 256 + found[2:3] * 65536


def weigh_kernel(
    share, length_ref, query_ref, fresh_key_ref, fresh_value_ref, left_ref, right_ref, place_ref,
    coarse_cos_ref, coarse_sin_ref, fine_cos_ref, fine_sin_ref,
    wire_ref, fresh_ref, raw_ref, score_ref, sent_ref,
):
    j = pl.program_id(0)
    in_block = pl.num_programs(0)
    heads, both, _ = query_ref.shape
    blocks = left_ref.shape[1]
    steps = place_ref.shape[1]
    group = both // steps
    holders = wire_ref.shape[0]
    half = HEAD_SIZE // 2
    scale = HEAD_SIZE ** (-0.5)

    raw_ref[...] = lax.dot_general(
        right_ref[...], left_ref[0], (((1,), (1,)), ((), ())), preferred_element_type=jnp.float32
    )
    fine_cos, fine_sin = fine_cos_ref[0], fine_sin_ref[0]
    cosine = coarse_cos_ref[...] * fine_cos - coarse_sin_ref[...] * fine_sin
    sine = coarse_sin_ref[...] * fine_cos + coarse_cos_ref[...] * fine_sin
    for head in range(heads):
        first = raw_ref[head * HEAD_SIZE : head * HEAD_SIZE + half]
        second = raw_ref[head * HEAD_SIZE + half : (head + 1) * HEAD_SIZE]
        keys = jnp.concatenate(
            [first * cosine - second * sine, second * cosine + first * sine], 0
        ).astype(jnp.bfloat16)
        score_ref[head, j] = (
            jnp.dot(query_ref[head], keys, preferred_element_type=jnp.float32) * scale
        )

    @pl.when(j == in_block - 1)
    def _():
        length = length_ref[0]
        tokens = score_ref.shape[1]
        block_at = lax.broadcasted_iota(jnp.int32, (both, blocks), 1)
        slot_at = lax.broadcasted_iota(jnp.int32, (holders * share, blocks), 0)
        fresh_keep = (
            lax.broadcasted_iota(jnp.int32, (both, 8), 1)
            <= lax.broadcasted_iota(jnp.int32, (both, 8), 0) // group
        )

        def one_head(head, _):
            query = query_ref[head]
            place = place_ref[head]
            place_rows = jnp.concatenate(
                [jnp.broadcast_to(place[s : s + 1], (group, blocks)) for s in range(steps)], 0
            )
            inside_at = jnp.where(place_rows >= 0, block_at * tokens, length)
            scores = [
                jnp.where(inside_at + t < length, score_ref[head, t], -jnp.inf)
                for t in range(tokens)
            ]
            fresh = lax.dot_general(
                query, fresh_key_ref[head], (((1,), (1,)), ((), ())),
                preferred_element_type=jnp.float32,
            ) * scale
            fresh = jnp.where(fresh_keep, fresh, -jnp.inf)
            top = scores[0]
            for t in range(1, tokens):
                top = jnp.maximum(top, scores[t])
            highest = jnp.maximum(
                jnp.max(top, -1, keepdims=True), jnp.max(fresh, -1, keepdims=True)
            )
            powers = [jnp.exp(score - highest) for score in scores]
            fresh_power = jnp.exp(fresh - highest)
            total = powers[0]
            for t in range(1, tokens):
                total = total + powers[t]
            denominator = jnp.sum(total, -1, keepdims=True) + jnp.sum(
                fresh_power, -1, keepdims=True
            )
            weights = [power / denominator for power in powers]
            fresh_weight = (fresh_power / denominator).astype(jnp.bfloat16)
            fresh_ref[head] = jnp.dot(
                fresh_weight, fresh_value_ref[head], preferred_element_type=jnp.float32
            )
            for s in range(steps):
                table = jnp.where(place[s : s + 1] == slot_at, 1.0, 0.0).astype(jnp.bfloat16)
                stacked = jnp.concatenate(
                    [weight[s * group : (s + 1) * group] for weight in weights], 0
                ).astype(jnp.bfloat16)
                routed = lax.dot_general(
                    table, stacked, (((1,), (1,)), ((), ())), preferred_element_type=jnp.float32
                )
                at = pl.multiple_of((s * heads + head) * share, share)
                sent_ref[:, pl.ds(at, share), :] = routed.reshape(holders, share, tokens * group)
            return 0

        lax.fori_loop(0, heads, one_head, 0)
        for holder in range(holders):
            wire_ref[holder] = sent_ref[holder].T.astype(jnp.bfloat16)


def meet_kernel(
    share, wire_ref, fresh_ref, tiles_ref, out_ref,
    got_ref, part_ref, back_ref, block_ref,
    tile_sem, weight_send, weight_recv, part_send, part_recv,
):
    holders, lines, lanes = wire_ref.shape
    rows = out_ref.shape[0]
    in_block = block_ref.shape[2] // HEAD_SIZE
    group = lines // in_block
    me = lax.axis_index("store")

    def tile_copy(k):
        source = lax.rem(me - k + holders, holders)
        return pltpu.make_async_copy(
            tiles_ref.at[pl.ds(pl.multiple_of(source * lanes, lanes), lanes)],
            block_ref.at[k],
            tile_sem.at[k],
        )

    def weight_copy(k):
        peer = lax.rem(me + k, holders)
        return pltpu.make_async_remote_copy(
            src_ref=wire_ref.at[peer],
            dst_ref=got_ref.at[k],
            send_sem=weight_send.at[k],
            recv_sem=weight_recv.at[k],
            device_id={"store": peer},
            device_id_type=pl.DeviceIdType.MESH,
        )

    def part_copy(k):
        peer = lax.rem(me - k + holders, holders)
        return pltpu.make_async_remote_copy(
            src_ref=part_ref.at[k],
            dst_ref=back_ref.at[k],
            send_sem=part_send.at[k],
            recv_sem=part_recv.at[k],
            device_id={"store": peer},
            device_id_type=pl.DeviceIdType.MESH,
        )

    barrier = pltpu.get_barrier_semaphore()

    def greet(k, _):
        pl.semaphore_signal(
            barrier, inc=1, device_id={"store": lax.rem(me + k, holders)},
            device_id_type=pl.DeviceIdType.MESH,
        )
        return 0

    lax.fori_loop(1, holders, greet, 0)
    for k in range(holders):
        tile_copy(k).start()
    pl.semaphore_wait(barrier, holders - 1)
    for k in range(1, holders):
        weight_copy(k).start()

    same = (
        lax.broadcasted_iota(jnp.int32, (rows, lanes), 0) // group
        == lax.broadcasted_iota(jnp.int32, (rows, lanes), 1) // share
    )

    def partial(weight, k):
        total = jnp.zeros((rows, HEAD_SIZE), jnp.float32)
        weight = weight.astype(jnp.float32)
        for j in range(in_block):
            piece = weight[j * group : (j + 1) * group]
            spread = jnp.where(same, jnp.concatenate([piece] * (rows // group), 0), 0.0)
            total = total + jnp.dot(
                spread.astype(jnp.bfloat16),
                block_ref[k, :, j * HEAD_SIZE : (j + 1) * HEAD_SIZE],
                preferred_element_type=jnp.float32,
            )
        return total

    tile_copy(0).wait()
    own = partial(wire_ref[me], 0) + fresh_ref[...]

    def answer(k, _):
        tile_copy(k).wait()
        weight_copy(k).wait_recv()
        part_ref[k] = partial(got_ref[k], k).astype(jnp.bfloat16)
        part_copy(k).start()
        return 0

    lax.fori_loop(1, holders, answer, 0)

    def collect(k, total):
        part_copy(k).wait_recv()
        return total + back_ref[k].astype(jnp.float32)

    out_ref[...] = lax.fori_loop(1, holders, collect, own).astype(jnp.bfloat16)

    def finish(k, _):
        weight_copy(k).wait_send()
        part_copy(k).wait_send()
        return 0

    lax.fori_loop(1, holders, finish, 0)


def routed_device(
    queries, new_keys, incoming_values, key_left, right_key_factor, value_tile_store, slot_map,
    chosen, lengths,
):
    holders = lax.axis_size("store")
    steps, _, heads, picks = chosen.shape
    blocks = slot_map.shape[2]
    share = max(1, blocks // holders // 4)
    pool_here = value_tile_store.shape[0]
    group = queries.shape[2] // HEAD_SIZE // heads
    rank = key_left.shape[2]
    slots = steps * heads * share
    total = holders * share
    keeper = slot_map[0] // pool_here
    inside = slot_map[0] % pool_here
    place, request = pl.pallas_call(
        functools.partial(plan_kernel, share),
        out_shape=(
            jax.ShapeDtypeStruct((steps * heads, blocks), jnp.int32),
            jax.ShapeDtypeStruct((steps * heads, total), jnp.int32),
        ),
        name="plan",
    )(chosen[:, 0].reshape(steps * heads, picks), keeper, inside)
    request = request.reshape(steps * heads, holders, share).transpose(1, 0, 2)
    asked = lax.all_to_all(
        request.reshape(holders, slots), "store", split_axis=0, concat_axis=0, tiled=True
    )

    length = lengths[0]
    query = apply_rotary(
        queries[:, 0].reshape(steps, heads * group, HEAD_SIZE).astype(jnp.float32),
        (length + jnp.arange(steps, dtype=jnp.int32))[:, None],
    ).astype(jnp.bfloat16)
    query = query.reshape(steps, heads, group, HEAD_SIZE).transpose(1, 0, 2, 3)
    query = query.reshape(heads, steps * group, HEAD_SIZE)
    fresh_key = apply_rotary(
        new_keys[:, 0].reshape(steps, heads, HEAD_SIZE).astype(jnp.float32),
        (length + jnp.arange(steps, dtype=jnp.int32))[:, None],
    ).astype(jnp.bfloat16)
    extra = ((0, 0), (0, 8 - steps), (0, 0))
    fresh_key = jnp.pad(fresh_key.transpose(1, 0, 2), extra)
    fresh_value = jnp.pad(
        incoming_values[:, 0].reshape(steps, heads, HEAD_SIZE).transpose(1, 0, 2), extra
    )
    left = key_left[0].reshape(blocks, BLOCK_TOKENS, rank).transpose(1, 0, 2)

    half = HEAD_SIZE // 2
    inverse = ROPE_BASE ** (-(np.arange(half, dtype=np.float32) * 2.0 / HEAD_SIZE))
    coarse = inverse[:, None] * (np.arange(blocks) * BLOCK_TOKENS)[None, :]
    fine = (np.arange(BLOCK_TOKENS)[:, None] * inverse[None, :])[..., None]
    constant = lambda table: jnp.asarray(table.astype(np.float32))
    whole = lambda *shape: pl.BlockSpec(shape, lambda j: (0,) * len(shape))
    per_token = lambda *shape: pl.BlockSpec((1,) + shape, lambda j: (j, 0, 0))
    wire, fresh = pl.pallas_call(
        functools.partial(weigh_kernel, share),
        grid=(BLOCK_TOKENS,),
        in_specs=[
            pl.BlockSpec(memory_space=pltpu.SMEM),
            whole(heads, steps * group, HEAD_SIZE),
            whole(heads, 8, HEAD_SIZE),
            whole(heads, 8, HEAD_SIZE),
            per_token(blocks, rank),
            whole(heads * HEAD_SIZE, rank),
            whole(heads, steps, blocks),
            whole(half, blocks),
            whole(half, blocks),
            per_token(half, 1),
            per_token(half, 1),
        ],
        out_specs=(
            whole(holders, BLOCK_TOKENS * group, slots),
            whole(heads, steps * group, HEAD_SIZE),
        ),
        out_shape=(
            jax.ShapeDtypeStruct((holders, BLOCK_TOKENS * group, slots), jnp.bfloat16),
            jax.ShapeDtypeStruct((heads, steps * group, HEAD_SIZE), jnp.float32),
        ),
        scratch_shapes=[
            pltpu.VMEM((heads * HEAD_SIZE, blocks), jnp.float32),
            pltpu.VMEM((heads, BLOCK_TOKENS, steps * group, blocks), jnp.float32),
            pltpu.VMEM((holders, slots, BLOCK_TOKENS * group), jnp.float32),
        ],
        cost_estimate=pl.CostEstimate(
            flops=4 * heads * blocks * BLOCK_TOKENS * rank * HEAD_SIZE,
            bytes_accessed=8 << 20,
            transcendentals=0,
        ),
        name="weigh",
    )(
        lengths, query, fresh_key, fresh_value, left, right_key_factor[0].T,
        place.reshape(steps, heads, blocks).transpose(1, 0, 2),
        constant(np.cos(coarse)), constant(np.sin(coarse)),
        constant(np.cos(fine)), constant(np.sin(fine)),
    )
    tiles = value_tile_store.at[asked.reshape(-1)].get(mode="promise_in_bounds")
    rows = steps * heads * group
    fresh = fresh.reshape(heads, steps, group, HEAD_SIZE).transpose(1, 0, 2, 3)
    lines = BLOCK_TOKENS * group
    in_vmem = pl.BlockSpec(memory_space=pltpu.VMEM)
    attended = pl.pallas_call(
        functools.partial(meet_kernel, share),
        in_specs=[in_vmem, in_vmem, pl.BlockSpec(memory_space=pl.ANY)],
        out_specs=in_vmem,
        out_shape=jax.ShapeDtypeStruct((rows, HEAD_SIZE), jnp.bfloat16),
        scratch_shapes=[
            pltpu.VMEM((holders, lines, slots), jnp.bfloat16),
            pltpu.VMEM((holders, rows, HEAD_SIZE), jnp.bfloat16),
            pltpu.VMEM((holders, rows, HEAD_SIZE), jnp.bfloat16),
            pltpu.VMEM((holders, slots, BLOCK_TOKENS * HEAD_SIZE), jnp.bfloat16),
        ]
        + [pltpu.SemaphoreType.DMA((holders,))] * 5,
        compiler_params=pltpu.CompilerParams(collective_id=0, has_side_effects=True),
        name="meet",
    )(wire, fresh.reshape(rows, HEAD_SIZE), tiles)
    return attended.reshape(steps, 1, -1)


def solution(mesh):
    in_specs = (
        P(None, ("groups", "store"), None),
        P(None, ("groups", "store"), None),
        P(None, ("groups", "store"), None),
        P(("groups", "store"), None, None),
        P(("groups", "store"), None, None),
        P(("groups", "store"), None),
        P(("groups", "store"), None, None),
        P(None, ("groups", "store"), None, None),
        P(("groups", "store")),
    )
    out_specs = P(None, ("groups", "store"), None)
    def body(*args):
        share = max(1, args[6].shape[2] // mesh.shape["store"] // 4)
        return (routed_device if share == 8 else per_device)(*args)

    return jax.shard_map(
        body, mesh=mesh, in_specs=in_specs, out_specs=out_specs, check_vma=False
    )
```

```python
import functools

import jax
import jax.numpy as jnp
import numpy as np
from jax import lax
from jax.experimental import pallas as pl
from jax.experimental.pallas import tpu as pltpu
from jax.sharding import PartitionSpec as P

KEY_VALUE_HEADS = 8
HEAD_SIZE = 128
BLOCK_TOKENS = 8


ROPE_BASE = 500000.0


def apply_rotary(tensor, token_positions):
    half_dim = tensor.shape[-1] // 2
    inverse = ROPE_BASE ** (-(jnp.arange(half_dim, dtype=jnp.float32) * 2.0 / tensor.shape[-1]))
    angles = jnp.asarray(token_positions).astype(jnp.float32)[..., None] * inverse
    cosine = jnp.cos(angles)
    sine_vals = jnp.sin(angles)
    first_half = tensor[..., :half_dim]
    second_half = tensor[..., half_dim:]
    return jnp.concatenate(
        [
            first_half * cosine - second_half * sine_vals,
            second_half * cosine + first_half * sine_vals,
        ],
        -1,
    )


def fetch_tiles(requests, value_tile_store):
    tile_row_index = jnp.take(
        value_tile_store,
        lax.all_to_all(requests, "store", split_axis=0, concat_axis=0, tiled=True),
        axis=0,
    )
    return lax.all_to_all(tile_row_index, "store", split_axis=0, concat_axis=0, tiled=True)


def build_requests(flat_idx, inside, total):
    buffer = jnp.zeros((total,), jnp.int32)
    return buffer.at[flat_idx.reshape(-1)].set(inside.reshape(-1))


def attend_row(
    query_full,
    incoming_keys_full,
    incoming_values_full,
    left_rows,
    right_factor_rows,
    block_numbers,
    tile_row_index,
    length,
    step_index,
):
    query_group_size = query_full.shape[-1] // HEAD_SIZE // KEY_VALUE_HEADS
    every_head = query_group_size * KEY_VALUE_HEADS
    selected_count = block_numbers.shape[1]
    score_scale = HEAD_SIZE ** (-0.5)
    right_factor_heads = right_factor_rows.reshape(
        right_factor_rows.shape[0], KEY_VALUE_HEADS, HEAD_SIZE
    )
    token_positions = (
        block_numbers[:, :, None] * BLOCK_TOKENS + jnp.arange(BLOCK_TOKENS, dtype=jnp.int32)
    ).reshape(KEY_VALUE_HEADS, selected_count * BLOCK_TOKENS)
    picked = left_rows[token_positions]
    raw_keys = jnp.einsum(
        "htr,rhd->htd", picked, right_factor_heads, preferred_element_type=jnp.float32
    )
    cache_keys = apply_rotary(raw_keys, token_positions).astype(jnp.bfloat16)
    rotated_query = apply_rotary(
        query_full[step_index].reshape(every_head, HEAD_SIZE).astype(jnp.float32),
        length + step_index,
    ).astype(jnp.bfloat16)
    current_position = (length + jnp.arange(step_index + 1, dtype=jnp.int32))[:, None]
    current_keys = apply_rotary(
        incoming_keys_full[: step_index + 1]
        .reshape(step_index + 1, KEY_VALUE_HEADS, HEAD_SIZE)
        .astype(jnp.float32),
        current_position,
    ).astype(jnp.bfloat16)
    current_keys = jnp.transpose(current_keys, (1, 0, 2))
    current_values = jnp.transpose(
        incoming_values_full[: step_index + 1].reshape(step_index + 1, KEY_VALUE_HEADS, HEAD_SIZE),
        (1, 0, 2),
    )
    local_values = tile_row_index.reshape(KEY_VALUE_HEADS, selected_count * BLOCK_TOKENS, HEAD_SIZE)
    grouped_queries = rotated_query.reshape(KEY_VALUE_HEADS, query_group_size, HEAD_SIZE)
    cache_scores = (
        jnp.einsum("hgd,htd->hgt", grouped_queries, cache_keys, preferred_element_type=jnp.float32)
        * score_scale
    )
    inside_len = token_positions < length
    cache_scores = jnp.where(inside_len[:, None, :], cache_scores, -jnp.inf)
    fresh_scores = (
        jnp.einsum(
            "hgd,hnd->hgn", grouped_queries, current_keys, preferred_element_type=jnp.float32
        )
        * score_scale
    )
    highest = jnp.maximum(
        jnp.max(cache_scores, -1, keepdims=True), jnp.max(fresh_scores, -1, keepdims=True)
    )
    cache_exp = jnp.exp(cache_scores - highest)
    fresh_exp = jnp.exp(fresh_scores - highest)
    denominator = jnp.sum(cache_exp, -1, keepdims=True) + jnp.sum(fresh_exp, -1, keepdims=True)
    cache_weight = (cache_exp / denominator).astype(jnp.bfloat16)
    fresh_weight = (fresh_exp / denominator).astype(jnp.bfloat16)
    attended = jnp.einsum(
        "hgt,htd->hgd", cache_weight, local_values, preferred_element_type=jnp.float32
    )
    attended = attended + jnp.einsum(
        "hgn,hnd->hgd", fresh_weight, current_values, preferred_element_type=jnp.float32
    )
    return attended.reshape(every_head * HEAD_SIZE).astype(jnp.bfloat16)


def per_device(
    queries,
    new_keys,
    incoming_values,
    key_left,
    right_key_factor,
    value_tile_store,
    slot_map,
    chosen,
    lengths,
):
    nstore = lax.axis_size("store")
    local_rows = key_left.shape[0]
    nchunk = slot_map.shape[2]
    step_count = chosen.shape[0]
    selected_count = chosen.shape[3]
    keeper_share = max(1, nchunk // nstore // 4)
    tile_limit = local_rows * KEY_VALUE_HEADS * keeper_share
    pool_here = value_tile_store.shape[0]
    slot_numbers = jnp.take_along_axis(
        jnp.broadcast_to(slot_map[None], (step_count,) + slot_map.shape), chosen, axis=3
    )
    tile_keeper = slot_numbers // pool_here
    inside = slot_numbers % pool_here
    matched = tile_keeper[..., :, None] == tile_keeper[..., None, :]
    earlier = jnp.arange(selected_count)[None, :] < jnp.arange(selected_count)[:, None]
    order_in = jnp.sum(jnp.logical_and(matched, earlier), -1)
    row_head = (
        jnp.arange(local_rows, dtype=jnp.int32)[:, None, None] * KEY_VALUE_HEADS
        + jnp.arange(KEY_VALUE_HEADS, dtype=jnp.int32)[None, :, None]
    )
    position = row_head * keeper_share + order_in
    tiles_all = []
    slot_span = step_count * tile_limit
    flat_idx = (
        tile_keeper * slot_span
        + jnp.arange(step_count, dtype=jnp.int32)[:, None, None, None] * tile_limit
        + position
    )
    requests = build_requests(flat_idx, inside, nstore * slot_span).reshape(nstore, slot_span)
    received = fetch_tiles(requests, value_tile_store).reshape(nstore * slot_span, -1)
    for step_index in range(step_count):
        tiles_all.append(received[flat_idx[step_index]])
    results = []
    for step_index in range(step_count):
        per_rows = [
            attend_row(
                queries[:, 0],
                new_keys[:, 0],
                incoming_values[:, 0],
                key_left[0],
                right_key_factor[0],
                chosen[step_index, 0],
                tiles_all[step_index][0],
                lengths[0],
                step_index,
            )
        ]
        results.append(jnp.stack(per_rows))
    return jnp.stack(results)


def plan_kernel(share, chosen_ref, keeper_ref, inside_ref, place_ref, request_ref):
    rows, picks = chosen_ref.shape
    heads, blocks = keeper_ref.shape
    total = request_ref.shape[1]
    holders = total // share
    block_at = lax.broadcasted_iota(jnp.int32, (rows, blocks), 1)
    chosen = chosen_ref[...]
    hit = jnp.zeros((rows, blocks), jnp.int32)
    for pick in range(picks):
        hit = jnp.where(chosen[:, pick : pick + 1] == block_at, 1, hit)
    keeper = jnp.concatenate([keeper_ref[...]] * (rows // heads), 0)
    kept = jnp.where(hit == 1, keeper, -1)
    before = (
        lax.broadcasted_iota(jnp.int32, (blocks, blocks), 0)
        < lax.broadcasted_iota(jnp.int32, (blocks, blocks), 1)
    ).astype(jnp.float32).astype(jnp.bfloat16)
    mine = [jnp.where(kept == holder, 1.0, 0.0) for holder in range(holders)]
    counts = jnp.dot(
        jnp.concatenate(mine, 0).astype(jnp.bfloat16), before, preferred_element_type=jnp.float32
    )
    order = jnp.zeros((rows, blocks), jnp.float32)
    for holder in range(holders):
        order = order + mine[holder] * counts[holder * rows : (holder + 1) * rows]
    place = jnp.where(hit == 1, keeper * share + order.astype(jnp.int32), -1)
    place_ref[...] = place
    inside = inside_ref[...]
    low = (inside & 255).astype(jnp.float32)
    middle = ((inside >> 8) & 255).astype(jnp.float32)
    high = (inside >> 16).astype(jnp.float32)
    slot_at = lax.broadcasted_iota(jnp.int32, (total, blocks), 0)
    for row in range(rows):
        head = row % heads
        digits = jnp.concatenate(
            [low[head : head + 1], middle[head : head + 1], high[head : head + 1],
             jnp.zeros((5, blocks), jnp.float32)], 0
        ).astype(jnp.bfloat16)
        table = jnp.where(place[row : row + 1] == slot_at, 1.0, 0.0).astype(jnp.bfloat16)
        found = lax.dot_general(
            digits, table, (((1,), (1,)), ((), ())), preferred_element_type=jnp.float32
        ).astype(jnp.int32)
        request_ref[row : row + 1, :] = found[0:1] + found[1:2] * 256 + found[2:3] * 65536


def weigh_kernel(
    share, length_ref, query_ref, fresh_key_ref, fresh_value_ref, left_ref, right_ref, place_ref,
    coarse_cos_ref, coarse_sin_ref, fine_cos_ref, fine_sin_ref,
    wire_ref, fresh_ref, raw_ref, score_ref, sent_ref,
):
    j = pl.program_id(0)
    in_block = pl.num_programs(0)
    heads, both, _ = query_ref.shape
    blocks = left_ref.shape[1]
    steps = place_ref.shape[1]
    group = both // steps
    holders = wire_ref.shape[0]
    half = HEAD_SIZE // 2
    scale = HEAD_SIZE ** (-0.5)

    raw_ref[...] = lax.dot_general(
        right_ref[...], left_ref[0], (((1,), (1,)), ((), ())), preferred_element_type=jnp.float32
    )
    fine_cos, fine_sin = fine_cos_ref[0], fine_sin_ref[0]
    cosine = coarse_cos_ref[...] * fine_cos - coarse_sin_ref[...] * fine_sin
    sine = coarse_sin_ref[...] * fine_cos + coarse_cos_ref[...] * fine_sin
    for head in range(heads):
        first = raw_ref[head * HEAD_SIZE : head * HEAD_SIZE + half]
        second = raw_ref[head * HEAD_SIZE + half : (head + 1) * HEAD_SIZE]
        keys = jnp.concatenate(
            [first * cosine - second * sine, second * cosine + first * sine], 0
        ).astype(jnp.bfloat16)
        score_ref[head, j] = (
            jnp.dot(query_ref[head], keys, preferred_element_type=jnp.float32) * scale
        )

    @pl.when(j == in_block - 1)
    def _():
        length = length_ref[0]
        tokens = score_ref.shape[1]
        block_at = lax.broadcasted_iota(jnp.int32, (both, blocks), 1)
        slot_at = lax.broadcasted_iota(jnp.int32, (holders * share, blocks), 0)
        fresh_keep = (
            lax.broadcasted_iota(jnp.int32, (both, 8), 1)
            <= lax.broadcasted_iota(jnp.int32, (both, 8), 0) // group
        )

        def one_head(head, _):
            query = query_ref[head]
            place = place_ref[head]
            place_rows = jnp.concatenate(
                [jnp.broadcast_to(place[s : s + 1], (group, blocks)) for s in range(steps)], 0
            )
            inside_at = jnp.where(place_rows >= 0, block_at * tokens, length)
            scores = [
                jnp.where(inside_at + t < length, score_ref[head, t], -jnp.inf)
                for t in range(tokens)
            ]
            fresh = lax.dot_general(
                query, fresh_key_ref[head], (((1,), (1,)), ((), ())),
                preferred_element_type=jnp.float32,
            ) * scale
            fresh = jnp.where(fresh_keep, fresh, -jnp.inf)
            top = scores[0]
            for t in range(1, tokens):
                top = jnp.maximum(top, scores[t])
            highest = jnp.maximum(
                jnp.max(top, -1, keepdims=True), jnp.max(fresh, -1, keepdims=True)
            )
            powers = [jnp.exp(score - highest) for score in scores]
            fresh_power = jnp.exp(fresh - highest)
            total = powers[0]
            for t in range(1, tokens):
                total = total + powers[t]
            denominator = jnp.sum(total, -1, keepdims=True) + jnp.sum(
                fresh_power, -1, keepdims=True
            )
            weights = [power / denominator for power in powers]
            fresh_weight = (fresh_power / denominator).astype(jnp.bfloat16)
            fresh_part = jnp.dot(
                fresh_weight, fresh_value_ref[head], preferred_element_type=jnp.float32
            )
            for s in range(steps):
                fresh_ref[s, head] = fresh_part[s * group : (s + 1) * group]
            for s in range(steps):
                table = jnp.where(place[s : s + 1] == slot_at, 1.0, 0.0).astype(jnp.bfloat16)
                stacked = jnp.concatenate(
                    [weight[s * group : (s + 1) * group] for weight in weights], 0
                ).astype(jnp.bfloat16)
                routed = lax.dot_general(
                    table, stacked, (((1,), (1,)), ((), ())), preferred_element_type=jnp.float32
                )
                at = pl.multiple_of((s * heads + head) * share, share)
                sent_ref[:, pl.ds(at, share), :] = routed.reshape(holders, share, tokens * group)
            return 0

        lax.fori_loop(0, heads, one_head, 0)
        for holder in range(holders):
            wire_ref[holder] = sent_ref[holder].T.astype(jnp.bfloat16)


def meet_kernel(
    share, wire_ref, fresh_ref, tiles_ref, out_ref,
    got_ref, part_ref, back_ref, block_ref,
    tile_sem, weight_send, weight_recv, part_send, part_recv,
):
    holders, lines, lanes = wire_ref.shape
    rows = out_ref.shape[0]
    in_block = block_ref.shape[2] // HEAD_SIZE
    group = lines // in_block
    me = lax.axis_index("store")

    def tile_copy(k):
        source = lax.rem(me - k + holders, holders)
        return pltpu.make_async_copy(
            tiles_ref.at[pl.ds(pl.multiple_of(source * lanes, lanes), lanes)],
            block_ref.at[k],
            tile_sem.at[k],
        )

    def weight_copy(k):
        peer = lax.rem(me + k, holders)
        return pltpu.make_async_remote_copy(
            src_ref=wire_ref.at[peer],
            dst_ref=got_ref.at[k],
            send_sem=weight_send.at[k],
            recv_sem=weight_recv.at[k],
            device_id={"store": peer},
            device_id_type=pl.DeviceIdType.MESH,
        )

    def part_copy(k):
        peer = lax.rem(me - k + holders, holders)
        return pltpu.make_async_remote_copy(
            src_ref=part_ref.at[k],
            dst_ref=back_ref.at[k],
            send_sem=part_send.at[k],
            recv_sem=part_recv.at[k],
            device_id={"store": peer},
            device_id_type=pl.DeviceIdType.MESH,
        )

    barrier = pltpu.get_barrier_semaphore()

    def greet(k, _):
        pl.semaphore_signal(
            barrier, inc=1, device_id={"store": lax.rem(me + k, holders)},
            device_id_type=pl.DeviceIdType.MESH,
        )
        return 0

    lax.fori_loop(1, holders, greet, 0)
    far_first = sorted(range(1, holders), key=lambda k: abs(2 * k - holders))
    for k in [0] + far_first:
        tile_copy(k).start()
    pl.semaphore_wait(barrier, holders - 1)
    for k in far_first:
        weight_copy(k).start()

    same = (
        lax.broadcasted_iota(jnp.int32, (rows, lanes), 0) // group
        == lax.broadcasted_iota(jnp.int32, (rows, lanes), 1) // share
    )

    def partial(weight, k):
        weight = weight.astype(jnp.float32)
        spread = [
            jnp.where(
                same, jnp.concatenate([weight[j * group : (j + 1) * group]] * (rows // group), 0), 0.0
            ).astype(jnp.bfloat16)
            for j in range(in_block)
        ]
        values = [
            block_ref[k, :, j * HEAD_SIZE : (j + 1) * HEAD_SIZE] for j in range(in_block)
        ]
        return jnp.dot(
            jnp.concatenate(spread, 1),
            jnp.concatenate(values, 0),
            preferred_element_type=jnp.float32,
        )

    tile_copy(0).wait()
    own = partial(wire_ref[me], 0) + fresh_ref[...]

    for at in range(0, holders - 1, 3):
        trio = far_first[at : at + 3]
        for k in trio:
            tile_copy(k).wait()
            weight_copy(k).wait_recv()
        parts = [partial(got_ref[k], k).astype(jnp.bfloat16) for k in trio]
        for k, part in zip(trio, parts):
            part_ref[k] = part
        for k in trio:
            part_copy(k).start()

    def collect(k, total):
        part_copy(k).wait_recv()
        return total + back_ref[k].astype(jnp.float32)

    out_ref[...] = lax.fori_loop(1, holders, collect, own).astype(jnp.bfloat16)

    def finish(k, _):
        weight_copy(k).wait_send()
        part_copy(k).wait_send()
        return 0

    lax.fori_loop(1, holders, finish, 0)


def routed_device(
    queries, new_keys, incoming_values, key_left, right_key_factor, value_tile_store, slot_map,
    chosen, lengths,
):
    holders = lax.axis_size("store")
    steps, _, heads, picks = chosen.shape
    blocks = slot_map.shape[2]
    share = max(1, blocks // holders // 4)
    pool_here = value_tile_store.shape[0]
    group = queries.shape[2] // HEAD_SIZE // heads
    rank = key_left.shape[2]
    slots = steps * heads * share
    total = holders * share
    keeper = slot_map[0] // pool_here
    inside = slot_map[0] % pool_here
    place, request = pl.pallas_call(
        functools.partial(plan_kernel, share),
        out_shape=(
            jax.ShapeDtypeStruct((steps * heads, blocks), jnp.int32),
            jax.ShapeDtypeStruct((steps * heads, total), jnp.int32),
        ),
        name="plan",
    )(chosen[:, 0].reshape(steps * heads, picks), keeper, inside)
    request = request.reshape(steps * heads, holders, share).transpose(1, 0, 2)
    asked = lax.all_to_all(
        request.reshape(holders, slots), "store", split_axis=0, concat_axis=0, tiled=True
    )

    length = lengths[0]
    query = apply_rotary(
        queries[:, 0].reshape(steps, heads * group, HEAD_SIZE).astype(jnp.float32),
        (length + jnp.arange(steps, dtype=jnp.int32))[:, None],
    ).astype(jnp.bfloat16)
    query = query.reshape(steps, heads, group, HEAD_SIZE).transpose(1, 0, 2, 3)
    query = query.reshape(heads, steps * group, HEAD_SIZE)
    fresh_key = apply_rotary(
        new_keys[:, 0].reshape(steps, heads, HEAD_SIZE).astype(jnp.float32),
        (length + jnp.arange(steps, dtype=jnp.int32))[:, None],
    ).astype(jnp.bfloat16)
    extra = ((0, 0), (0, 8 - steps), (0, 0))
    fresh_key = jnp.pad(fresh_key.transpose(1, 0, 2), extra)
    fresh_value = jnp.pad(
        incoming_values[:, 0].reshape(steps, heads, HEAD_SIZE).transpose(1, 0, 2), extra
    )
    left = key_left[0].reshape(blocks, BLOCK_TOKENS, rank).transpose(1, 0, 2)

    half = HEAD_SIZE // 2
    inverse = ROPE_BASE ** (-(np.arange(half, dtype=np.float32) * 2.0 / HEAD_SIZE))
    coarse = inverse[:, None] * (np.arange(blocks) * BLOCK_TOKENS)[None, :]
    fine = (np.arange(BLOCK_TOKENS)[:, None] * inverse[None, :])[..., None]
    constant = lambda table: jnp.asarray(table.astype(np.float32))
    whole = lambda *shape: pl.BlockSpec(shape, lambda j: (0,) * len(shape))
    per_token = lambda *shape: pl.BlockSpec((1,) + shape, lambda j: (j, 0, 0))
    wire, fresh = pl.pallas_call(
        functools.partial(weigh_kernel, share),
        grid=(BLOCK_TOKENS,),
        in_specs=[
            pl.BlockSpec(memory_space=pltpu.SMEM),
            whole(heads, steps * group, HEAD_SIZE),
            whole(heads, 8, HEAD_SIZE),
            whole(heads, 8, HEAD_SIZE),
            per_token(blocks, rank),
            whole(heads * HEAD_SIZE, rank),
            whole(heads, steps, blocks),
            whole(half, blocks),
            whole(half, blocks),
            per_token(half, 1),
            per_token(half, 1),
        ],
        out_specs=(
            whole(holders, BLOCK_TOKENS * group, slots),
            whole(steps, heads, group, HEAD_SIZE),
        ),
        out_shape=(
            jax.ShapeDtypeStruct((holders, BLOCK_TOKENS * group, slots), jnp.bfloat16),
            jax.ShapeDtypeStruct((steps, heads, group, HEAD_SIZE), jnp.float32),
        ),
        scratch_shapes=[
            pltpu.VMEM((heads * HEAD_SIZE, blocks), jnp.float32),
            pltpu.VMEM((heads, BLOCK_TOKENS, steps * group, blocks), jnp.float32),
            pltpu.VMEM((holders, slots, BLOCK_TOKENS * group), jnp.float32),
        ],
        cost_estimate=pl.CostEstimate(
            flops=4 * heads * blocks * BLOCK_TOKENS * rank * HEAD_SIZE,
            bytes_accessed=8 << 20,
            transcendentals=0,
        ),
        name="weigh",
    )(
        lengths, query, fresh_key, fresh_value, left, right_key_factor[0].T,
        place.reshape(steps, heads, blocks).transpose(1, 0, 2),
        constant(np.cos(coarse)), constant(np.sin(coarse)),
        constant(np.cos(fine)), constant(np.sin(fine)),
    )
    tiles = value_tile_store.at[asked.reshape(-1)].get(mode="promise_in_bounds")
    rows = steps * heads * group
    lines = BLOCK_TOKENS * group
    in_vmem = pl.BlockSpec(memory_space=pltpu.VMEM)
    attended = pl.pallas_call(
        functools.partial(meet_kernel, share),
        in_specs=[in_vmem, in_vmem, pl.BlockSpec(memory_space=pl.ANY)],
        out_specs=in_vmem,
        out_shape=jax.ShapeDtypeStruct((rows, HEAD_SIZE), jnp.bfloat16),
        scratch_shapes=[
            pltpu.VMEM((holders, lines, slots), jnp.bfloat16),
            pltpu.VMEM((holders, rows, HEAD_SIZE), jnp.bfloat16),
            pltpu.VMEM((holders, rows, HEAD_SIZE), jnp.bfloat16),
            pltpu.VMEM((holders, slots, BLOCK_TOKENS * HEAD_SIZE), jnp.bfloat16),
        ]
        + [pltpu.SemaphoreType.DMA((holders,))] * 5,
        compiler_params=pltpu.CompilerParams(collective_id=0, has_side_effects=True),
        name="meet",
    )(wire, fresh.reshape(rows, HEAD_SIZE), tiles)
    return attended.reshape(steps, 1, -1)


def solution(mesh):
    in_specs = (
        P(None, ("groups", "store"), None),
        P(None, ("groups", "store"), None),
        P(None, ("groups", "store"), None),
        P(("groups", "store"), None, None),
        P(("groups", "store"), None, None),
        P(("groups", "store"), None),
        P(("groups", "store"), None, None),
        P(None, ("groups", "store"), None, None),
        P(("groups", "store")),
    )
    out_specs = P(None, ("groups", "store"), None)
    def body(*args):
        share = max(1, args[6].shape[2] // mesh.shape["store"] // 4)
        return (routed_device if share == 8 else per_device)(*args)

    return jax.shard_map(
        body, mesh=mesh, in_specs=in_specs, out_specs=out_specs, check_vma=False
    )
```

```python
import functools

import jax
import jax.numpy as jnp
import numpy as np
from jax import lax
from jax.experimental import pallas as pl
from jax.experimental.pallas import tpu as pltpu
from jax.sharding import PartitionSpec as P

KEY_VALUE_HEADS = 8
HEAD_SIZE = 128
BLOCK_TOKENS = 8


ROPE_BASE = 500000.0


def apply_rotary(tensor, token_positions):
    half_dim = tensor.shape[-1] // 2
    inverse = ROPE_BASE ** (-(jnp.arange(half_dim, dtype=jnp.float32) * 2.0 / tensor.shape[-1]))
    angles = jnp.asarray(token_positions).astype(jnp.float32)[..., None] * inverse
    cosine = jnp.cos(angles)
    sine_vals = jnp.sin(angles)
    first_half = tensor[..., :half_dim]
    second_half = tensor[..., half_dim:]
    return jnp.concatenate(
        [
            first_half * cosine - second_half * sine_vals,
            second_half * cosine + first_half * sine_vals,
        ],
        -1,
    )


def fetch_tiles(requests, value_tile_store):
    tile_row_index = jnp.take(
        value_tile_store,
        lax.all_to_all(requests, "store", split_axis=0, concat_axis=0, tiled=True),
        axis=0,
    )
    return lax.all_to_all(tile_row_index, "store", split_axis=0, concat_axis=0, tiled=True)


def build_requests(flat_idx, inside, total):
    buffer = jnp.zeros((total,), jnp.int32)
    return buffer.at[flat_idx.reshape(-1)].set(inside.reshape(-1))


def attend_row(
    query_full,
    incoming_keys_full,
    incoming_values_full,
    left_rows,
    right_factor_rows,
    block_numbers,
    tile_row_index,
    length,
    step_index,
):
    query_group_size = query_full.shape[-1] // HEAD_SIZE // KEY_VALUE_HEADS
    every_head = query_group_size * KEY_VALUE_HEADS
    selected_count = block_numbers.shape[1]
    score_scale = HEAD_SIZE ** (-0.5)
    right_factor_heads = right_factor_rows.reshape(
        right_factor_rows.shape[0], KEY_VALUE_HEADS, HEAD_SIZE
    )
    token_positions = (
        block_numbers[:, :, None] * BLOCK_TOKENS + jnp.arange(BLOCK_TOKENS, dtype=jnp.int32)
    ).reshape(KEY_VALUE_HEADS, selected_count * BLOCK_TOKENS)
    picked = left_rows[token_positions]
    raw_keys = jnp.einsum(
        "htr,rhd->htd", picked, right_factor_heads, preferred_element_type=jnp.float32
    )
    cache_keys = apply_rotary(raw_keys, token_positions).astype(jnp.bfloat16)
    rotated_query = apply_rotary(
        query_full[step_index].reshape(every_head, HEAD_SIZE).astype(jnp.float32),
        length + step_index,
    ).astype(jnp.bfloat16)
    current_position = (length + jnp.arange(step_index + 1, dtype=jnp.int32))[:, None]
    current_keys = apply_rotary(
        incoming_keys_full[: step_index + 1]
        .reshape(step_index + 1, KEY_VALUE_HEADS, HEAD_SIZE)
        .astype(jnp.float32),
        current_position,
    ).astype(jnp.bfloat16)
    current_keys = jnp.transpose(current_keys, (1, 0, 2))
    current_values = jnp.transpose(
        incoming_values_full[: step_index + 1].reshape(step_index + 1, KEY_VALUE_HEADS, HEAD_SIZE),
        (1, 0, 2),
    )
    local_values = tile_row_index.reshape(KEY_VALUE_HEADS, selected_count * BLOCK_TOKENS, HEAD_SIZE)
    grouped_queries = rotated_query.reshape(KEY_VALUE_HEADS, query_group_size, HEAD_SIZE)
    cache_scores = (
        jnp.einsum("hgd,htd->hgt", grouped_queries, cache_keys, preferred_element_type=jnp.float32)
        * score_scale
    )
    inside_len = token_positions < length
    cache_scores = jnp.where(inside_len[:, None, :], cache_scores, -jnp.inf)
    fresh_scores = (
        jnp.einsum(
            "hgd,hnd->hgn", grouped_queries, current_keys, preferred_element_type=jnp.float32
        )
        * score_scale
    )
    highest = jnp.maximum(
        jnp.max(cache_scores, -1, keepdims=True), jnp.max(fresh_scores, -1, keepdims=True)
    )
    cache_exp = jnp.exp(cache_scores - highest)
    fresh_exp = jnp.exp(fresh_scores - highest)
    denominator = jnp.sum(cache_exp, -1, keepdims=True) + jnp.sum(fresh_exp, -1, keepdims=True)
    cache_weight = (cache_exp / denominator).astype(jnp.bfloat16)
    fresh_weight = (fresh_exp / denominator).astype(jnp.bfloat16)
    attended = jnp.einsum(
        "hgt,htd->hgd", cache_weight, local_values, preferred_element_type=jnp.float32
    )
    attended = attended + jnp.einsum(
        "hgn,hnd->hgd", fresh_weight, current_values, preferred_element_type=jnp.float32
    )
    return attended.reshape(every_head * HEAD_SIZE).astype(jnp.bfloat16)


def per_device(
    queries,
    new_keys,
    incoming_values,
    key_left,
    right_key_factor,
    value_tile_store,
    slot_map,
    chosen,
    lengths,
):
    nstore = lax.axis_size("store")
    local_rows = key_left.shape[0]
    nchunk = slot_map.shape[2]
    step_count = chosen.shape[0]
    selected_count = chosen.shape[3]
    keeper_share = max(1, nchunk // nstore // 4)
    tile_limit = local_rows * KEY_VALUE_HEADS * keeper_share
    pool_here = value_tile_store.shape[0]
    slot_numbers = jnp.take_along_axis(
        jnp.broadcast_to(slot_map[None], (step_count,) + slot_map.shape), chosen, axis=3
    )
    tile_keeper = slot_numbers // pool_here
    inside = slot_numbers % pool_here
    matched = tile_keeper[..., :, None] == tile_keeper[..., None, :]
    earlier = jnp.arange(selected_count)[None, :] < jnp.arange(selected_count)[:, None]
    order_in = jnp.sum(jnp.logical_and(matched, earlier), -1)
    row_head = (
        jnp.arange(local_rows, dtype=jnp.int32)[:, None, None] * KEY_VALUE_HEADS
        + jnp.arange(KEY_VALUE_HEADS, dtype=jnp.int32)[None, :, None]
    )
    position = row_head * keeper_share + order_in
    tiles_all = []
    slot_span = step_count * tile_limit
    flat_idx = (
        tile_keeper * slot_span
        + jnp.arange(step_count, dtype=jnp.int32)[:, None, None, None] * tile_limit
        + position
    )
    requests = build_requests(flat_idx, inside, nstore * slot_span).reshape(nstore, slot_span)
    received = fetch_tiles(requests, value_tile_store).reshape(nstore * slot_span, -1)
    for step_index in range(step_count):
        tiles_all.append(received[flat_idx[step_index]])
    results = []
    for step_index in range(step_count):
        per_rows = [
            attend_row(
                queries[:, 0],
                new_keys[:, 0],
                incoming_values[:, 0],
                key_left[0],
                right_key_factor[0],
                chosen[step_index, 0],
                tiles_all[step_index][0],
                lengths[0],
                step_index,
            )
        ]
        results.append(jnp.stack(per_rows))
    return jnp.stack(results)


def plan_kernel(
    share, chosen_ref, keeper_ref, inside_ref, place_ref, asked_ref,
    send_ref, recv_ref, send_sem, recv_sem,
):
    me = lax.axis_index("store")
    count = asked_ref.shape[0]
    barrier = pltpu.get_barrier_semaphore()

    def greet(k, _):
        pl.semaphore_signal(
            barrier, inc=1, device_id={"store": lax.rem(me + k, count)},
            device_id_type=pl.DeviceIdType.MESH,
        )
        return 0

    lax.fori_loop(1, count, greet, 0)
    rows, picks = chosen_ref.shape
    heads, blocks = keeper_ref.shape
    holders = count
    total = holders * share
    block_at = lax.broadcasted_iota(jnp.int32, (rows, blocks), 1)
    chosen = chosen_ref[...]
    hit = jnp.zeros((rows, blocks), jnp.int32)
    for pick in range(picks):
        hit = jnp.where(chosen[:, pick : pick + 1] == block_at, 1, hit)
    keeper = jnp.concatenate([keeper_ref[...]] * (rows // heads), 0)
    kept = jnp.where(hit == 1, keeper, -1)
    before = (
        lax.broadcasted_iota(jnp.int32, (blocks, blocks), 0)
        < lax.broadcasted_iota(jnp.int32, (blocks, blocks), 1)
    ).astype(jnp.float32).astype(jnp.bfloat16)
    mine = [jnp.where(kept == holder, 1.0, 0.0) for holder in range(holders)]
    counts = jnp.dot(
        jnp.concatenate(mine, 0).astype(jnp.bfloat16), before, preferred_element_type=jnp.float32
    )
    order = jnp.zeros((rows, blocks), jnp.float32)
    for holder in range(holders):
        order = order + mine[holder] * counts[holder * rows : (holder + 1) * rows]
    place = jnp.where(hit == 1, keeper * share + order.astype(jnp.int32), -1)
    place_ref[...] = place
    inside = inside_ref[...]
    low = (inside & 255).astype(jnp.float32)
    middle = ((inside >> 8) & 255).astype(jnp.float32)
    high = (inside >> 16).astype(jnp.float32)
    slot_at = lax.broadcasted_iota(jnp.int32, (total, blocks), 0)
    moved = []
    for row in range(rows):
        head = row % heads
        digits = jnp.concatenate(
            [low[head : head + 1], middle[head : head + 1], high[head : head + 1],
             jnp.zeros((5, blocks), jnp.float32)], 0
        ).astype(jnp.bfloat16)
        table = jnp.where(place[row : row + 1] == slot_at, 1.0, 0.0).astype(jnp.bfloat16)
        found = lax.dot_general(
            digits, table, (((1,), (1,)), ((), ())), preferred_element_type=jnp.float32
        ).astype(jnp.int32)
        found = found[0:1] + found[1:2] * 256 + found[2:3] * 65536
        moved.append(pltpu.roll(found, row * share, 1) if row else found)
    moved = jnp.concatenate(moved, 0)
    own_lanes = (
        lax.broadcasted_iota(jnp.int32, (rows, total), 1) // share
        == lax.broadcasted_iota(jnp.int32, (rows, total), 0)
    )
    for holder in range(holders):
        turned = pltpu.roll(moved, total - holder * share, 1) if holder else moved
        send_ref[holder] = jnp.sum(jnp.where(own_lanes, turned, 0), 0, keepdims=True)

    def copy(k):
        peer = lax.rem(me + k, holders)
        return pltpu.make_async_remote_copy(
            src_ref=send_ref.at[peer],
            dst_ref=recv_ref.at[k],
            send_sem=send_sem.at[k],
            recv_sem=recv_sem.at[k],
            device_id={"store": peer},
            device_id_type=pl.DeviceIdType.MESH,
        )

    pl.semaphore_wait(barrier, holders - 1)
    for k in range(1, holders):
        copy(k).start()
    asked_ref[0] = send_ref[me]
    for k in range(1, holders):
        copy(k).wait_recv()
        asked_ref[k] = recv_ref[k]
    for k in range(1, holders):
        copy(k).wait_send()


def weigh_kernel(
    share, length_ref, query_ref, fresh_key_ref, fresh_value_ref, left_ref, right_ref, place_ref,
    coarse_cos_ref, coarse_sin_ref, fine_cos_ref, fine_sin_ref,
    wire_ref, fresh_ref, raw_ref, score_ref, sent_ref,
):
    j = pl.program_id(0)
    in_block = pl.num_programs(0)
    heads, both, _ = query_ref.shape
    blocks = left_ref.shape[1]
    steps = place_ref.shape[1]
    group = both // steps
    holders = wire_ref.shape[0]
    half = HEAD_SIZE // 2
    scale = HEAD_SIZE ** (-0.5)

    raw_ref[...] = lax.dot_general(
        right_ref[...], left_ref[0], (((1,), (1,)), ((), ())), preferred_element_type=jnp.float32
    )
    fine_cos, fine_sin = fine_cos_ref[0], fine_sin_ref[0]
    cosine = coarse_cos_ref[...] * fine_cos - coarse_sin_ref[...] * fine_sin
    sine = coarse_sin_ref[...] * fine_cos + coarse_cos_ref[...] * fine_sin
    for head in range(heads):
        first = raw_ref[head * HEAD_SIZE : head * HEAD_SIZE + half]
        second = raw_ref[head * HEAD_SIZE + half : (head + 1) * HEAD_SIZE]
        keys = jnp.concatenate(
            [first * cosine - second * sine, second * cosine + first * sine], 0
        ).astype(jnp.bfloat16)
        score_ref[head, j] = (
            jnp.dot(query_ref[head], keys, preferred_element_type=jnp.float32) * scale
        )

    @pl.when(j == in_block - 1)
    def _():
        length = length_ref[0]
        tokens = score_ref.shape[1]
        block_at = lax.broadcasted_iota(jnp.int32, (both, blocks), 1)
        slot_at = lax.broadcasted_iota(jnp.int32, (holders * share, blocks), 0)
        fresh_keep = (
            lax.broadcasted_iota(jnp.int32, (both, 8), 1)
            <= lax.broadcasted_iota(jnp.int32, (both, 8), 0) // group
        )

        def one_head(head, _):
            query = query_ref[head]
            place = place_ref[head]
            place_rows = jnp.concatenate(
                [jnp.broadcast_to(place[s : s + 1], (group, blocks)) for s in range(steps)], 0
            )
            inside_at = jnp.where(place_rows >= 0, block_at * tokens, length)
            scores = [
                jnp.where(inside_at + t < length, score_ref[head, t], -jnp.inf)
                for t in range(tokens)
            ]
            fresh = lax.dot_general(
                query, fresh_key_ref[head], (((1,), (1,)), ((), ())),
                preferred_element_type=jnp.float32,
            ) * scale
            fresh = jnp.where(fresh_keep, fresh, -jnp.inf)
            top = scores[0]
            for t in range(1, tokens):
                top = jnp.maximum(top, scores[t])
            highest = jnp.maximum(
                jnp.max(top, -1, keepdims=True), jnp.max(fresh, -1, keepdims=True)
            )
            powers = [jnp.exp(score - highest) for score in scores]
            fresh_power = jnp.exp(fresh - highest)
            total = powers[0]
            for t in range(1, tokens):
                total = total + powers[t]
            denominator = jnp.sum(total, -1, keepdims=True) + jnp.sum(
                fresh_power, -1, keepdims=True
            )
            weights = [power / denominator for power in powers]
            fresh_weight = (fresh_power / denominator).astype(jnp.bfloat16)
            fresh_part = jnp.dot(
                fresh_weight, fresh_value_ref[head], preferred_element_type=jnp.float32
            )
            for s in range(steps):
                fresh_ref[s, head] = fresh_part[s * group : (s + 1) * group]
            for s in range(steps):
                table = jnp.where(place[s : s + 1] == slot_at, 1.0, 0.0).astype(jnp.bfloat16)
                stacked = jnp.concatenate(
                    [weight[s * group : (s + 1) * group] for weight in weights], 0
                ).astype(jnp.bfloat16)
                routed = lax.dot_general(
                    table, stacked, (((1,), (1,)), ((), ())), preferred_element_type=jnp.float32
                )
                at = pl.multiple_of((s * heads + head) * share, share)
                sent_ref[:, pl.ds(at, share), :] = routed.reshape(holders, share, tokens * group)
            return 0

        lax.fori_loop(0, heads, one_head, 0)
        for holder in range(holders):
            wire_ref[holder] = sent_ref[holder].T.astype(jnp.bfloat16)


def meet_kernel(
    share, wire_ref, fresh_ref, tiles_ref, out_ref,
    got_ref, part_ref, back_ref, block_ref,
    tile_sem, weight_send, weight_recv, part_send, part_recv,
):
    holders, lines, lanes = wire_ref.shape
    rows = out_ref.shape[0]
    in_block = block_ref.shape[2] // HEAD_SIZE
    group = lines // in_block
    me = lax.axis_index("store")

    def tile_copy(k):
        return pltpu.make_async_copy(
            tiles_ref.at[pl.ds(k * lanes, lanes)],
            block_ref.at[k],
            tile_sem.at[k],
        )

    def weight_copy(k):
        peer = lax.rem(me + k, holders)
        return pltpu.make_async_remote_copy(
            src_ref=wire_ref.at[peer],
            dst_ref=got_ref.at[k],
            send_sem=weight_send.at[k],
            recv_sem=weight_recv.at[k],
            device_id={"store": peer},
            device_id_type=pl.DeviceIdType.MESH,
        )

    def part_copy(k):
        peer = lax.rem(me - k + holders, holders)
        return pltpu.make_async_remote_copy(
            src_ref=part_ref.at[k],
            dst_ref=back_ref.at[k],
            send_sem=part_send.at[k],
            recv_sem=part_recv.at[k],
            device_id={"store": peer},
            device_id_type=pl.DeviceIdType.MESH,
        )

    barrier = pltpu.get_barrier_semaphore()

    def greet(k, _):
        pl.semaphore_signal(
            barrier, inc=1, device_id={"store": lax.rem(me + k, holders)},
            device_id_type=pl.DeviceIdType.MESH,
        )
        return 0

    lax.fori_loop(1, holders, greet, 0)
    far_first = sorted(range(1, holders), key=lambda k: abs(2 * k - holders))
    for k in [0] + far_first:
        tile_copy(k).start()
    pl.semaphore_wait(barrier, holders - 1)
    for k in far_first:
        weight_copy(k).start()

    same = (
        lax.broadcasted_iota(jnp.int32, (rows, lanes), 0) // group
        == lax.broadcasted_iota(jnp.int32, (rows, lanes), 1) // share
    )

    def partial(weight, k):
        weight = weight.astype(jnp.float32)
        spread = [
            jnp.where(
                same, jnp.concatenate([weight[j * group : (j + 1) * group]] * (rows // group), 0), 0.0
            ).astype(jnp.bfloat16)
            for j in range(in_block)
        ]
        values = [
            block_ref[k, :, j * HEAD_SIZE : (j + 1) * HEAD_SIZE] for j in range(in_block)
        ]
        return jnp.dot(
            jnp.concatenate(spread, 1),
            jnp.concatenate(values, 0),
            preferred_element_type=jnp.float32,
        )

    tile_copy(0).wait()
    own = partial(wire_ref[me], 0) + fresh_ref[...]

    for at in range(0, holders - 1, 3):
        trio = far_first[at : at + 3]
        for k in trio:
            tile_copy(k).wait()
            weight_copy(k).wait_recv()
        parts = [partial(got_ref[k], k).astype(jnp.bfloat16) for k in trio]
        for k, part in zip(trio, parts):
            part_ref[k] = part
        for k in trio:
            part_copy(k).start()

    def collect(k, total):
        part_copy(k).wait_recv()
        return total + back_ref[k].astype(jnp.float32)

    out_ref[...] = lax.fori_loop(1, holders, collect, own).astype(jnp.bfloat16)

    def finish(k, _):
        weight_copy(k).wait_send()
        part_copy(k).wait_send()
        return 0

    lax.fori_loop(1, holders, finish, 0)


def routed_device(
    queries, new_keys, incoming_values, key_left, right_key_factor, value_tile_store, slot_map,
    chosen, lengths,
):
    holders = lax.axis_size("store")
    steps, _, heads, picks = chosen.shape
    blocks = slot_map.shape[2]
    share = max(1, blocks // holders // 4)
    pool_here = value_tile_store.shape[0]
    group = queries.shape[2] // HEAD_SIZE // heads
    rank = key_left.shape[2]
    slots = steps * heads * share
    keeper = slot_map[0] // pool_here
    inside = slot_map[0] % pool_here
    place, asked = pl.pallas_call(
        functools.partial(plan_kernel, share),
        out_shape=(
            jax.ShapeDtypeStruct((steps * heads, blocks), jnp.int32),
            jax.ShapeDtypeStruct((holders, 1, slots), jnp.int32),
        ),
        scratch_shapes=[
            pltpu.VMEM((holders, 1, slots), jnp.int32),
            pltpu.VMEM((holders, 1, slots), jnp.int32),
            pltpu.SemaphoreType.DMA((holders,)),
            pltpu.SemaphoreType.DMA((holders,)),
        ],
        compiler_params=pltpu.CompilerParams(collective_id=1, has_side_effects=True),
        name="plan",
    )(chosen[:, 0].reshape(steps * heads, picks), keeper, inside)

    length = lengths[0]
    query = apply_rotary(
        queries[:, 0].reshape(steps, heads * group, HEAD_SIZE).astype(jnp.float32),
        (length + jnp.arange(steps, dtype=jnp.int32))[:, None],
    ).astype(jnp.bfloat16)
    query = query.reshape(steps, heads, group, HEAD_SIZE).transpose(1, 0, 2, 3)
    query = query.reshape(heads, steps * group, HEAD_SIZE)
    fresh_key = apply_rotary(
        new_keys[:, 0].reshape(steps, heads, HEAD_SIZE).astype(jnp.float32),
        (length + jnp.arange(steps, dtype=jnp.int32))[:, None],
    ).astype(jnp.bfloat16)
    extra = ((0, 0), (0, 8 - steps), (0, 0))
    fresh_key = jnp.pad(fresh_key.transpose(1, 0, 2), extra)
    fresh_value = jnp.pad(
        incoming_values[:, 0].reshape(steps, heads, HEAD_SIZE).transpose(1, 0, 2), extra
    )
    left = key_left[0].reshape(blocks, BLOCK_TOKENS, rank).transpose(1, 0, 2)

    half = HEAD_SIZE // 2
    inverse = ROPE_BASE ** (-(np.arange(half, dtype=np.float32) * 2.0 / HEAD_SIZE))
    coarse = inverse[:, None] * (np.arange(blocks) * BLOCK_TOKENS)[None, :]
    fine = (np.arange(BLOCK_TOKENS)[:, None] * inverse[None, :])[..., None]
    constant = lambda table: jnp.asarray(table.astype(np.float32))
    whole = lambda *shape: pl.BlockSpec(shape, lambda j: (0,) * len(shape))
    per_token = lambda *shape: pl.BlockSpec((1,) + shape, lambda j: (j, 0, 0))
    wire, fresh = pl.pallas_call(
        functools.partial(weigh_kernel, share),
        grid=(BLOCK_TOKENS,),
        in_specs=[
            pl.BlockSpec(memory_space=pltpu.SMEM),
            whole(heads, steps * group, HEAD_SIZE),
            whole(heads, 8, HEAD_SIZE),
            whole(heads, 8, HEAD_SIZE),
            per_token(blocks, rank),
            whole(heads * HEAD_SIZE, rank),
            whole(heads, steps, blocks),
            whole(half, blocks),
            whole(half, blocks),
            per_token(half, 1),
            per_token(half, 1),
        ],
        out_specs=(
            whole(holders, BLOCK_TOKENS * group, slots),
            whole(steps, heads, group, HEAD_SIZE),
        ),
        out_shape=(
            jax.ShapeDtypeStruct((holders, BLOCK_TOKENS * group, slots), jnp.bfloat16),
            jax.ShapeDtypeStruct((steps, heads, group, HEAD_SIZE), jnp.float32),
        ),
        scratch_shapes=[
            pltpu.VMEM((heads * HEAD_SIZE, blocks), jnp.float32),
            pltpu.VMEM((heads, BLOCK_TOKENS, steps * group, blocks), jnp.float32),
            pltpu.VMEM((holders, slots, BLOCK_TOKENS * group), jnp.float32),
        ],
        cost_estimate=pl.CostEstimate(
            flops=4 * heads * blocks * BLOCK_TOKENS * rank * HEAD_SIZE,
            bytes_accessed=8 << 20,
            transcendentals=0,
        ),
        name="weigh",
    )(
        lengths, query, fresh_key, fresh_value, left, right_key_factor[0].T,
        place.reshape(steps, heads, blocks).transpose(1, 0, 2),
        constant(np.cos(coarse)), constant(np.sin(coarse)),
        constant(np.cos(fine)), constant(np.sin(fine)),
    )
    tiles = value_tile_store.at[asked.reshape(-1)].get(mode="promise_in_bounds")
    rows = steps * heads * group
    lines = BLOCK_TOKENS * group
    in_vmem = pl.BlockSpec(memory_space=pltpu.VMEM)
    attended = pl.pallas_call(
        functools.partial(meet_kernel, share),
        in_specs=[in_vmem, in_vmem, pl.BlockSpec(memory_space=pl.ANY)],
        out_specs=in_vmem,
        out_shape=jax.ShapeDtypeStruct((rows, HEAD_SIZE), jnp.bfloat16),
        scratch_shapes=[
            pltpu.VMEM((holders, lines, slots), jnp.bfloat16),
            pltpu.VMEM((holders, rows, HEAD_SIZE), jnp.bfloat16),
            pltpu.VMEM((holders, rows, HEAD_SIZE), jnp.bfloat16),
            pltpu.VMEM((holders, slots, BLOCK_TOKENS * HEAD_SIZE), jnp.bfloat16),
        ]
        + [pltpu.SemaphoreType.DMA((holders,))] * 5,
        compiler_params=pltpu.CompilerParams(collective_id=0, has_side_effects=True),
        name="meet",
    )(wire, fresh.reshape(rows, HEAD_SIZE), tiles)
    return attended.reshape(steps, 1, -1)


def solution(mesh):
    in_specs = (
        P(None, ("groups", "store"), None),
        P(None, ("groups", "store"), None),
        P(None, ("groups", "store"), None),
        P(("groups", "store"), None, None),
        P(("groups", "store"), None, None),
        P(("groups", "store"), None),
        P(("groups", "store"), None, None),
        P(None, ("groups", "store"), None, None),
        P(("groups", "store")),
    )
    out_specs = P(None, ("groups", "store"), None)
    def body(*args):
        share = max(1, args[6].shape[2] // mesh.shape["store"] // 4)
        square = args[7].shape[0] * args[7].shape[2] == mesh.shape["store"]
        return (routed_device if share == 8 and square else per_device)(*args)

    return jax.shard_map(
        body, mesh=mesh, in_specs=in_specs, out_specs=out_specs, check_vma=False
    )
```

```python
import functools

import jax
import jax.numpy as jnp
import numpy as np
from jax import lax
from jax.experimental import pallas as pl
from jax.experimental.pallas import tpu as pltpu
from jax.sharding import PartitionSpec as P

KEY_VALUE_HEADS = 8
HEAD_SIZE = 128
BLOCK_TOKENS = 8


ROPE_BASE = 500000.0


def apply_rotary(tensor, token_positions):
    half_dim = tensor.shape[-1] // 2
    inverse = ROPE_BASE ** (-(jnp.arange(half_dim, dtype=jnp.float32) * 2.0 / tensor.shape[-1]))
    angles = jnp.asarray(token_positions).astype(jnp.float32)[..., None] * inverse
    cosine = jnp.cos(angles)
    sine_vals = jnp.sin(angles)
    first_half = tensor[..., :half_dim]
    second_half = tensor[..., half_dim:]
    return jnp.concatenate(
        [
            first_half * cosine - second_half * sine_vals,
            second_half * cosine + first_half * sine_vals,
        ],
        -1,
    )


def fetch_tiles(requests, value_tile_store):
    tile_row_index = jnp.take(
        value_tile_store,
        lax.all_to_all(requests, "store", split_axis=0, concat_axis=0, tiled=True),
        axis=0,
    )
    return lax.all_to_all(tile_row_index, "store", split_axis=0, concat_axis=0, tiled=True)


def build_requests(flat_idx, inside, total):
    buffer = jnp.zeros((total,), jnp.int32)
    return buffer.at[flat_idx.reshape(-1)].set(inside.reshape(-1))


def attend_row(
    query_full,
    incoming_keys_full,
    incoming_values_full,
    left_rows,
    right_factor_rows,
    block_numbers,
    tile_row_index,
    length,
    step_index,
):
    query_group_size = query_full.shape[-1] // HEAD_SIZE // KEY_VALUE_HEADS
    every_head = query_group_size * KEY_VALUE_HEADS
    selected_count = block_numbers.shape[1]
    score_scale = HEAD_SIZE ** (-0.5)
    right_factor_heads = right_factor_rows.reshape(
        right_factor_rows.shape[0], KEY_VALUE_HEADS, HEAD_SIZE
    )
    token_positions = (
        block_numbers[:, :, None] * BLOCK_TOKENS + jnp.arange(BLOCK_TOKENS, dtype=jnp.int32)
    ).reshape(KEY_VALUE_HEADS, selected_count * BLOCK_TOKENS)
    picked = left_rows[token_positions]
    raw_keys = jnp.einsum(
        "htr,rhd->htd", picked, right_factor_heads, preferred_element_type=jnp.float32
    )
    cache_keys = apply_rotary(raw_keys, token_positions).astype(jnp.bfloat16)
    rotated_query = apply_rotary(
        query_full[step_index].reshape(every_head, HEAD_SIZE).astype(jnp.float32),
        length + step_index,
    ).astype(jnp.bfloat16)
    current_position = (length + jnp.arange(step_index + 1, dtype=jnp.int32))[:, None]
    current_keys = apply_rotary(
        incoming_keys_full[: step_index + 1]
        .reshape(step_index + 1, KEY_VALUE_HEADS, HEAD_SIZE)
        .astype(jnp.float32),
        current_position,
    ).astype(jnp.bfloat16)
    current_keys = jnp.transpose(current_keys, (1, 0, 2))
    current_values = jnp.transpose(
        incoming_values_full[: step_index + 1].reshape(step_index + 1, KEY_VALUE_HEADS, HEAD_SIZE),
        (1, 0, 2),
    )
    local_values = tile_row_index.reshape(KEY_VALUE_HEADS, selected_count * BLOCK_TOKENS, HEAD_SIZE)
    grouped_queries = rotated_query.reshape(KEY_VALUE_HEADS, query_group_size, HEAD_SIZE)
    cache_scores = (
        jnp.einsum("hgd,htd->hgt", grouped_queries, cache_keys, preferred_element_type=jnp.float32)
        * score_scale
    )
    inside_len = token_positions < length
    cache_scores = jnp.where(inside_len[:, None, :], cache_scores, -jnp.inf)
    fresh_scores = (
        jnp.einsum(
            "hgd,hnd->hgn", grouped_queries, current_keys, preferred_element_type=jnp.float32
        )
        * score_scale
    )
    highest = jnp.maximum(
        jnp.max(cache_scores, -1, keepdims=True), jnp.max(fresh_scores, -1, keepdims=True)
    )
    cache_exp = jnp.exp(cache_scores - highest)
    fresh_exp = jnp.exp(fresh_scores - highest)
    denominator = jnp.sum(cache_exp, -1, keepdims=True) + jnp.sum(fresh_exp, -1, keepdims=True)
    cache_weight = (cache_exp / denominator).astype(jnp.bfloat16)
    fresh_weight = (fresh_exp / denominator).astype(jnp.bfloat16)
    attended = jnp.einsum(
        "hgt,htd->hgd", cache_weight, local_values, preferred_element_type=jnp.float32
    )
    attended = attended + jnp.einsum(
        "hgn,hnd->hgd", fresh_weight, current_values, preferred_element_type=jnp.float32
    )
    return attended.reshape(every_head * HEAD_SIZE).astype(jnp.bfloat16)


def per_device(
    queries,
    new_keys,
    incoming_values,
    key_left,
    right_key_factor,
    value_tile_store,
    slot_map,
    chosen,
    lengths,
):
    nstore = lax.axis_size("store")
    local_rows = key_left.shape[0]
    nchunk = slot_map.shape[2]
    step_count = chosen.shape[0]
    selected_count = chosen.shape[3]
    keeper_share = max(1, nchunk // nstore // 4)
    tile_limit = local_rows * KEY_VALUE_HEADS * keeper_share
    pool_here = value_tile_store.shape[0]
    slot_numbers = jnp.take_along_axis(
        jnp.broadcast_to(slot_map[None], (step_count,) + slot_map.shape), chosen, axis=3
    )
    tile_keeper = slot_numbers // pool_here
    inside = slot_numbers % pool_here
    matched = tile_keeper[..., :, None] == tile_keeper[..., None, :]
    earlier = jnp.arange(selected_count)[None, :] < jnp.arange(selected_count)[:, None]
    order_in = jnp.sum(jnp.logical_and(matched, earlier), -1)
    row_head = (
        jnp.arange(local_rows, dtype=jnp.int32)[:, None, None] * KEY_VALUE_HEADS
        + jnp.arange(KEY_VALUE_HEADS, dtype=jnp.int32)[None, :, None]
    )
    position = row_head * keeper_share + order_in
    tiles_all = []
    slot_span = step_count * tile_limit
    flat_idx = (
        tile_keeper * slot_span
        + jnp.arange(step_count, dtype=jnp.int32)[:, None, None, None] * tile_limit
        + position
    )
    requests = build_requests(flat_idx, inside, nstore * slot_span).reshape(nstore, slot_span)
    received = fetch_tiles(requests, value_tile_store).reshape(nstore * slot_span, -1)
    for step_index in range(step_count):
        tiles_all.append(received[flat_idx[step_index]])
    results = []
    for step_index in range(step_count):
        per_rows = [
            attend_row(
                queries[:, 0],
                new_keys[:, 0],
                incoming_values[:, 0],
                key_left[0],
                right_key_factor[0],
                chosen[step_index, 0],
                tiles_all[step_index][0],
                lengths[0],
                step_index,
            )
        ]
        results.append(jnp.stack(per_rows))
    return jnp.stack(results)


def plan_kernel(
    share, chosen_ref, keeper_ref, inside_ref, place_ref, asked_ref,
    send_ref, recv_ref, send_sem, recv_sem,
):
    me = lax.axis_index("store")
    count = asked_ref.shape[0]
    barrier = pltpu.get_barrier_semaphore()

    def greet(k, _):
        pl.semaphore_signal(
            barrier, inc=1, device_id={"store": lax.rem(me + k, count)},
            device_id_type=pl.DeviceIdType.MESH,
        )
        return 0

    lax.fori_loop(1, count, greet, 0)
    rows, picks = chosen_ref.shape
    heads, blocks = keeper_ref.shape
    holders = count
    total = holders * share
    block_at = lax.broadcasted_iota(jnp.int32, (rows, blocks), 1)
    chosen = chosen_ref[...]
    hit = jnp.zeros((rows, blocks), jnp.int32)
    for pick in range(picks):
        hit = jnp.where(chosen[:, pick : pick + 1] == block_at, 1, hit)
    keeper = jnp.concatenate([keeper_ref[...]] * (rows // heads), 0)
    kept = jnp.where(hit == 1, keeper, -1)
    before = (
        lax.broadcasted_iota(jnp.int32, (blocks, blocks), 0)
        < lax.broadcasted_iota(jnp.int32, (blocks, blocks), 1)
    ).astype(jnp.float32).astype(jnp.bfloat16)
    mine = [jnp.where(kept == holder, 1.0, 0.0) for holder in range(holders)]
    counts = jnp.dot(
        jnp.concatenate(mine, 0).astype(jnp.bfloat16), before, preferred_element_type=jnp.float32
    )
    order = jnp.zeros((rows, blocks), jnp.float32)
    for holder in range(holders):
        order = order + mine[holder] * counts[holder * rows : (holder + 1) * rows]
    place = jnp.where(hit == 1, keeper * share + order.astype(jnp.int32), -1)
    place_ref[...] = place
    inside = inside_ref[...]
    low = (inside & 255).astype(jnp.float32)
    middle = ((inside >> 8) & 255).astype(jnp.float32)
    high = (inside >> 16).astype(jnp.float32)
    slot_at = lax.broadcasted_iota(jnp.int32, (total, blocks), 0)
    moved = []
    for row in range(rows):
        head = row % heads
        digits = jnp.concatenate(
            [low[head : head + 1], middle[head : head + 1], high[head : head + 1],
             jnp.zeros((5, blocks), jnp.float32)], 0
        ).astype(jnp.bfloat16)
        table = jnp.where(place[row : row + 1] == slot_at, 1.0, 0.0).astype(jnp.bfloat16)
        found = lax.dot_general(
            digits, table, (((1,), (1,)), ((), ())), preferred_element_type=jnp.float32
        ).astype(jnp.int32)
        found = found[0:1] + found[1:2] * 256 + found[2:3] * 65536
        moved.append(pltpu.roll(found, row * share, 1) if row else found)
    moved = jnp.concatenate(moved, 0)
    own_lanes = (
        lax.broadcasted_iota(jnp.int32, (rows, total), 1) // share
        == lax.broadcasted_iota(jnp.int32, (rows, total), 0)
    )
    for holder in range(holders):
        turned = pltpu.roll(moved, total - holder * share, 1) if holder else moved
        send_ref[holder] = jnp.sum(jnp.where(own_lanes, turned, 0), 0, keepdims=True)

    def copy(k):
        peer = lax.rem(me + k, holders)
        return pltpu.make_async_remote_copy(
            src_ref=send_ref.at[peer],
            dst_ref=recv_ref.at[k],
            send_sem=send_sem.at[k],
            recv_sem=recv_sem.at[k],
            device_id={"store": peer},
            device_id_type=pl.DeviceIdType.MESH,
        )

    pl.semaphore_wait(barrier, holders - 1)
    for k in range(1, holders):
        copy(k).start()
    asked_ref[0] = send_ref[me]
    for k in range(1, holders):
        copy(k).wait_recv()
        asked_ref[k] = recv_ref[k]
    for k in range(1, holders):
        copy(k).wait_send()


def weigh_kernel(
    share, length_ref, query_ref, fresh_key_ref, fresh_value_ref, left_ref, right_ref, place_ref,
    coarse_cos_ref, coarse_sin_ref, fine_cos_ref, fine_sin_ref,
    wire_ref, fresh_ref, raw_ref, score_ref, sent_ref,
):
    j = pl.program_id(0)
    in_block = pl.num_programs(0)
    heads, both, _ = query_ref.shape
    blocks = left_ref.shape[1]
    steps = place_ref.shape[0] // heads
    group = both // steps
    holders = wire_ref.shape[0]
    half = HEAD_SIZE // 2
    scale = HEAD_SIZE ** (-0.5)

    raw_ref[...] = lax.dot_general(
        right_ref[...], left_ref[0], (((1,), (1,)), ((), ())), preferred_element_type=jnp.float32
    )
    fine_cos, fine_sin = fine_cos_ref[0], fine_sin_ref[0]
    cosine = coarse_cos_ref[...] * fine_cos - coarse_sin_ref[...] * fine_sin
    sine = coarse_sin_ref[...] * fine_cos + coarse_cos_ref[...] * fine_sin
    for head in range(heads):
        first = raw_ref[head * HEAD_SIZE : head * HEAD_SIZE + half]
        second = raw_ref[head * HEAD_SIZE + half : (head + 1) * HEAD_SIZE]
        keys = jnp.concatenate(
            [first * cosine - second * sine, second * cosine + first * sine], 0
        ).astype(jnp.bfloat16)
        score_ref[head, j] = (
            jnp.dot(query_ref[head], keys, preferred_element_type=jnp.float32) * scale
        )

    @pl.when(j == in_block - 1)
    def _():
        length = length_ref[0]
        tokens = score_ref.shape[1]
        block_at = lax.broadcasted_iota(jnp.int32, (both, blocks), 1)
        slot_at = lax.broadcasted_iota(jnp.int32, (holders * share, blocks), 0)
        fresh_keep = (
            lax.broadcasted_iota(jnp.int32, (both, 8), 1)
            <= lax.broadcasted_iota(jnp.int32, (both, 8), 0) // group
        )

        def one_head(head, _):
            query = query_ref[head]
            place = jnp.concatenate(
                [place_ref[pl.ds(s * heads + head, 1)] for s in range(steps)], 0
            )
            place_rows = jnp.concatenate(
                [jnp.broadcast_to(place[s : s + 1], (group, blocks)) for s in range(steps)], 0
            )
            inside_at = jnp.where(place_rows >= 0, block_at * tokens, length)
            scores = [
                jnp.where(inside_at + t < length, score_ref[head, t], -jnp.inf)
                for t in range(tokens)
            ]
            fresh = lax.dot_general(
                query, fresh_key_ref[head], (((1,), (1,)), ((), ())),
                preferred_element_type=jnp.float32,
            ) * scale
            fresh = jnp.where(fresh_keep, fresh, -jnp.inf)
            top = scores[0]
            for t in range(1, tokens):
                top = jnp.maximum(top, scores[t])
            highest = jnp.maximum(
                jnp.max(top, -1, keepdims=True), jnp.max(fresh, -1, keepdims=True)
            )
            powers = [jnp.exp(score - highest) for score in scores]
            fresh_power = jnp.exp(fresh - highest)
            total = powers[0]
            for t in range(1, tokens):
                total = total + powers[t]
            denominator = jnp.sum(total, -1, keepdims=True) + jnp.sum(
                fresh_power, -1, keepdims=True
            )
            weights = [power / denominator for power in powers]
            fresh_weight = (fresh_power / denominator).astype(jnp.bfloat16)
            fresh_part = jnp.dot(
                fresh_weight, fresh_value_ref[head], preferred_element_type=jnp.float32
            )
            for s in range(steps):
                fresh_ref[s, head] = fresh_part[s * group : (s + 1) * group]
            for s in range(steps):
                table = jnp.where(place[s : s + 1] == slot_at, 1.0, 0.0).astype(jnp.bfloat16)
                stacked = jnp.concatenate(
                    [weight[s * group : (s + 1) * group] for weight in weights], 0
                ).astype(jnp.bfloat16)
                routed = lax.dot_general(
                    table, stacked, (((1,), (1,)), ((), ())), preferred_element_type=jnp.float32
                )
                at = pl.multiple_of((s * heads + head) * share, share)
                sent_ref[:, pl.ds(at, share), :] = routed.reshape(holders, share, tokens * group)
            return 0

        lax.fori_loop(0, heads, one_head, 0)
        for holder in range(holders):
            wire_ref[holder] = sent_ref[holder].T.astype(jnp.bfloat16)


def meet_kernel(
    share, wire_ref, fresh_ref, tiles_ref, out_ref,
    got_ref, part_ref, back_ref, block_ref,
    tile_sem, weight_send, weight_recv, part_send, part_recv,
):
    holders, lines, lanes = wire_ref.shape
    rows = out_ref.shape[0]
    in_block = block_ref.shape[2] // HEAD_SIZE
    group = lines // in_block
    me = lax.axis_index("store")

    def tile_copy(k):
        return pltpu.make_async_copy(
            tiles_ref.at[pl.ds(k * lanes, lanes)],
            block_ref.at[k],
            tile_sem.at[k],
        )

    def weight_copy(k):
        peer = lax.rem(me + k, holders)
        return pltpu.make_async_remote_copy(
            src_ref=wire_ref.at[peer],
            dst_ref=got_ref.at[k],
            send_sem=weight_send.at[k],
            recv_sem=weight_recv.at[k],
            device_id={"store": peer},
            device_id_type=pl.DeviceIdType.MESH,
        )

    def part_copy(k):
        peer = lax.rem(me - k + holders, holders)
        return pltpu.make_async_remote_copy(
            src_ref=part_ref.at[k],
            dst_ref=back_ref.at[k],
            send_sem=part_send.at[k],
            recv_sem=part_recv.at[k],
            device_id={"store": peer},
            device_id_type=pl.DeviceIdType.MESH,
        )

    barrier = pltpu.get_barrier_semaphore()

    def greet(k, _):
        pl.semaphore_signal(
            barrier, inc=1, device_id={"store": lax.rem(me + k, holders)},
            device_id_type=pl.DeviceIdType.MESH,
        )
        return 0

    lax.fori_loop(1, holders, greet, 0)
    far_first = sorted(range(1, holders), key=lambda k: abs(2 * k - holders))
    for k in [0] + far_first:
        tile_copy(k).start()
    pl.semaphore_wait(barrier, holders - 1)
    for k in far_first:
        weight_copy(k).start()

    same = (
        lax.broadcasted_iota(jnp.int32, (rows, lanes), 0) // group
        == lax.broadcasted_iota(jnp.int32, (rows, lanes), 1) // share
    )

    def partial(weight, k):
        weight = weight.astype(jnp.float32)
        spread = [
            jnp.where(
                same, jnp.concatenate([weight[j * group : (j + 1) * group]] * (rows // group), 0), 0.0
            ).astype(jnp.bfloat16)
            for j in range(in_block)
        ]
        values = [
            block_ref[k, :, j * HEAD_SIZE : (j + 1) * HEAD_SIZE] for j in range(in_block)
        ]
        return jnp.dot(
            jnp.concatenate(spread, 1),
            jnp.concatenate(values, 0),
            preferred_element_type=jnp.float32,
        )

    tile_copy(0).wait()
    own = partial(wire_ref[me], 0) + fresh_ref[...]

    for at in range(0, holders - 1, 3):
        trio = far_first[at : at + 3]
        for k in trio:
            tile_copy(k).wait()
            weight_copy(k).wait_recv()
        parts = [partial(got_ref[k], k).astype(jnp.bfloat16) for k in trio]
        for k, part in zip(trio, parts):
            part_ref[k] = part
        for k in trio:
            part_copy(k).start()

    def collect(k, total):
        part_copy(k).wait_recv()
        return total + back_ref[k].astype(jnp.float32)

    out_ref[...] = lax.fori_loop(1, holders, collect, own).astype(jnp.bfloat16)

    def finish(k, _):
        weight_copy(k).wait_send()
        part_copy(k).wait_send()
        return 0

    lax.fori_loop(1, holders, finish, 0)


def routed_device(
    queries, new_keys, incoming_values, key_left, right_key_factor, value_tile_store, slot_map,
    chosen, lengths,
):
    holders = lax.axis_size("store")
    steps, _, heads, picks = chosen.shape
    blocks = slot_map.shape[2]
    share = max(1, blocks // holders // 4)
    pool_here = value_tile_store.shape[0]
    group = queries.shape[2] // HEAD_SIZE // heads
    rank = key_left.shape[2]
    slots = steps * heads * share
    keeper = slot_map[0] // pool_here
    inside = slot_map[0] % pool_here
    place, asked = pl.pallas_call(
        functools.partial(plan_kernel, share),
        out_shape=(
            jax.ShapeDtypeStruct((steps * heads, blocks), jnp.int32),
            jax.ShapeDtypeStruct((holders, 1, slots), jnp.int32),
        ),
        scratch_shapes=[
            pltpu.VMEM((holders, 1, slots), jnp.int32),
            pltpu.VMEM((holders, 1, slots), jnp.int32),
            pltpu.SemaphoreType.DMA((holders,)),
            pltpu.SemaphoreType.DMA((holders,)),
        ],
        compiler_params=pltpu.CompilerParams(collective_id=1, has_side_effects=True),
        name="plan",
    )(chosen[:, 0].reshape(steps * heads, picks), keeper, inside)

    length = lengths[0]
    query = apply_rotary(
        queries[:, 0].reshape(steps, heads * group, HEAD_SIZE).astype(jnp.float32),
        (length + jnp.arange(steps, dtype=jnp.int32))[:, None],
    ).astype(jnp.bfloat16)
    query = query.reshape(steps, heads, group, HEAD_SIZE).transpose(1, 0, 2, 3)
    query = query.reshape(heads, steps * group, HEAD_SIZE)
    fresh_key = apply_rotary(
        new_keys[:, 0].reshape(steps, heads, HEAD_SIZE).astype(jnp.float32),
        (length + jnp.arange(steps, dtype=jnp.int32))[:, None],
    ).astype(jnp.bfloat16)
    extra = ((0, 0), (0, 8 - steps), (0, 0))
    fresh_key = jnp.pad(fresh_key.transpose(1, 0, 2), extra)
    fresh_value = jnp.pad(
        incoming_values[:, 0].reshape(steps, heads, HEAD_SIZE).transpose(1, 0, 2), extra
    )
    left = key_left[0].reshape(blocks, BLOCK_TOKENS, rank).transpose(1, 0, 2)

    half = HEAD_SIZE // 2
    inverse = ROPE_BASE ** (-(np.arange(half, dtype=np.float32) * 2.0 / HEAD_SIZE))
    coarse = inverse[:, None] * (np.arange(blocks) * BLOCK_TOKENS)[None, :]
    fine = (np.arange(BLOCK_TOKENS)[:, None] * inverse[None, :])[..., None]
    constant = lambda table: jnp.asarray(table.astype(np.float32))
    whole = lambda *shape: pl.BlockSpec(shape, lambda j: (0,) * len(shape))
    per_token = lambda *shape: pl.BlockSpec((1,) + shape, lambda j: (j, 0, 0))
    wire, fresh = pl.pallas_call(
        functools.partial(weigh_kernel, share),
        grid=(BLOCK_TOKENS,),
        in_specs=[
            pl.BlockSpec(memory_space=pltpu.SMEM),
            whole(heads, steps * group, HEAD_SIZE),
            whole(heads, 8, HEAD_SIZE),
            whole(heads, 8, HEAD_SIZE),
            per_token(blocks, rank),
            whole(heads * HEAD_SIZE, rank),
            whole(steps * heads, blocks),
            whole(half, blocks),
            whole(half, blocks),
            per_token(half, 1),
            per_token(half, 1),
        ],
        out_specs=(
            whole(holders, BLOCK_TOKENS * group, slots),
            whole(steps, heads, group, HEAD_SIZE),
        ),
        out_shape=(
            jax.ShapeDtypeStruct((holders, BLOCK_TOKENS * group, slots), jnp.bfloat16),
            jax.ShapeDtypeStruct((steps, heads, group, HEAD_SIZE), jnp.float32),
        ),
        scratch_shapes=[
            pltpu.VMEM((heads * HEAD_SIZE, blocks), jnp.float32),
            pltpu.VMEM((heads, BLOCK_TOKENS, steps * group, blocks), jnp.float32),
            pltpu.VMEM((holders, slots, BLOCK_TOKENS * group), jnp.float32),
        ],
        cost_estimate=pl.CostEstimate(
            flops=4 * heads * blocks * BLOCK_TOKENS * rank * HEAD_SIZE,
            bytes_accessed=8 << 20,
            transcendentals=0,
        ),
        name="weigh",
    )(
        lengths, query, fresh_key, fresh_value, left, right_key_factor[0].T,
        place,
        constant(np.cos(coarse)), constant(np.sin(coarse)),
        constant(np.cos(fine)), constant(np.sin(fine)),
    )
    tiles = value_tile_store.at[asked.reshape(-1)].get(mode="promise_in_bounds")
    rows = steps * heads * group
    lines = BLOCK_TOKENS * group
    in_vmem = pl.BlockSpec(memory_space=pltpu.VMEM)
    attended = pl.pallas_call(
        functools.partial(meet_kernel, share),
        in_specs=[in_vmem, in_vmem, pl.BlockSpec(memory_space=pl.ANY)],
        out_specs=in_vmem,
        out_shape=jax.ShapeDtypeStruct((rows, HEAD_SIZE), jnp.bfloat16),
        scratch_shapes=[
            pltpu.VMEM((holders, lines, slots), jnp.bfloat16),
            pltpu.VMEM((holders, rows, HEAD_SIZE), jnp.bfloat16),
            pltpu.VMEM((holders, rows, HEAD_SIZE), jnp.bfloat16),
            pltpu.VMEM((holders, slots, BLOCK_TOKENS * HEAD_SIZE), jnp.bfloat16),
        ]
        + [pltpu.SemaphoreType.DMA((holders,))] * 5,
        compiler_params=pltpu.CompilerParams(collective_id=0, has_side_effects=True),
        name="meet",
    )(wire, fresh.reshape(rows, HEAD_SIZE), tiles)
    return attended.reshape(steps, 1, -1)


def solution(mesh):
    in_specs = (
        P(None, ("groups", "store"), None),
        P(None, ("groups", "store"), None),
        P(None, ("groups", "store"), None),
        P(("groups", "store"), None, None),
        P(("groups", "store"), None, None),
        P(("groups", "store"), None),
        P(("groups", "store"), None, None),
        P(None, ("groups", "store"), None, None),
        P(("groups", "store")),
    )
    out_specs = P(None, ("groups", "store"), None)
    def body(*args):
        share = max(1, args[6].shape[2] // mesh.shape["store"] // 4)
        square = args[7].shape[0] * args[7].shape[2] == mesh.shape["store"]
        return (routed_device if share == 8 and square else per_device)(*args)

    return jax.shard_map(
        body, mesh=mesh, in_specs=in_specs, out_specs=out_specs, check_vma=False
    )
```
